32 devices in a mesh: gx: 4 (over x, core), gy: 8 (over z, y).
Axes of the slice: x: 2, y: 2, z: 4, core: 2. Of those that a mesh axis runs over, the one named last changes fastest.
Arguments:
- volume: bfloat16 [16, 64, 16, 128], P('gx', 'gy'), may hold values from -6 to 6
- basin_mask: int32 [16, 64, 32], P('gx', 'gy'), may hold values 0 or 1
- w_first: bfloat16 [27, 64, 128], replicated, may hold values from -0.15625 to 0.15625
- b_first: float32 [128], replicated, may hold values from -3 to 3
- w_second: bfloat16 [27, 128, 128], replicated, may hold values from -0.109375 to 0.109375
- b_second: float32 [128], replicated, may hold values from -3 to 3
- upstream: bfloat16 [16, 64, 32, 128], P('gx', 'gy'), may hold values from -6 to 6
Outputs:
- features: bfloat16 [16, 64, 32, 128], P('gx', 'gy')
- step_first: float32 [27, 64, 128], replicated
- step_second: float32 [27, 128, 128], replicated
The draws below stay inside these ranges and needn't reach their ends.
Inputs may be any that keep to these rules, and one draw needn't show every extreme that they name: basin_mask holds only 0 and 1.
All inputs are finite; a program needn't handle non-finite values. No bound on the sum of `basin_mask` on one device may be relied on, other than what follows from the above.
Results may differ from the reference program's by a relative error of at most 0.0054.
Values may be sent and summed in bfloat16 or wider, within the bound.
No kernel may reach another device: no remote copies, remote signals or barrier semaphores. Data moves between devices by JAX's collectives and lax.ppermute only.
A program may use at most 64 MiB of HBM per device.

```python
import jax
import jax.numpy as jnp
from jax import lax

CIN = 64
COUT = 128
NX = 16
NY = 64
NZ = 32


def plant(result, own_key, least, high):
    longest = result.shape.index(max(result.shape))
    spots = []
    for shift in (0, 1):
        where = [jax.random.randint(jax.random.fold_in(own_key, axis), (), 0, length) for axis, length in enumerate(result.shape)]
        where[longest] = (where[longest] + shift) % result.shape[longest]
        spots.append(tuple(where))
    return result.at[spots[0]].set(least).at[spots[1]].set(high)


def levels(own_key, extent, shards, low, largest):
    def one(dim, shards_of):
        draws = jax.random.uniform(jax.random.fold_in(jax.random.fold_in(own_key, 6), dim), (shards_of,), jnp.float32, low / len(shards), largest / len(shards))
        return jnp.repeat(jnp.exp(draws), extent[dim] // shards_of).reshape((-1,) + (1,) * (len(extent) - dim - 1))

    loudness = one(*shards[0])
    for cut in shards[1:]:
        loudness = loudness * one(*cut)
    return loudness


def normal_values(key, extent, spread, limit, cuts=(), kind=jnp.bfloat16):
    factor_of = levels(key, extent, cuts, -0.22, 0.18) if cuts else 1.0
    drawn = jax.random.normal(key, extent, jnp.float32) * spread * factor_of
    return jnp.minimum(jnp.maximum(drawn, -limit), limit).astype(kind)


def setup_inputs(seed: int = 0) -> dict:
    streams_of = jax.random.split(jax.random.key(seed), 8)
    return {
        "volume": normal_values(streams_of[0], (NX, NY, NZ // 2, 2 * CIN), 1.0, 6.0, ((0, 4), (1, 8))),
        "basin_mask": plant((jax.random.randint(streams_of[1], (NX, NY, NZ), 0, 4) < 3).astype(jnp.int32), jax.random.fold_in(streams_of[1], 1), 0, 1),
        "w_first": normal_values(streams_of[2], (27, CIN, COUT), (27 * CIN) ** -0.5, 0.15625),
        "b_first": normal_values(streams_of[3], (COUT,), 0.5, 3.0, (), jnp.float32),
        "w_second": normal_values(streams_of[4], (27, COUT, COUT), (27 * COUT) ** -0.5, 0.109375),
        "b_second": normal_values(streams_of[5], (COUT,), 0.5, 3.0, (), jnp.float32),
        "upstream": normal_values(streams_of[6], (NX, NY, NZ, COUT), 1.0, 6.0, ((0, 4), (1, 8))),
    }


def windowed(padded, tap, size_x, size_y, size_z):
    tap_x = tap // 9
    tap_y = tap // 3 % 3
    tap_z = tap % 3
    window = padded[tap_x:tap_x + size_x, tap_y:tap_y + size_y, tap_z:tap_z + size_z]
    return window.reshape(-1, padded.shape[3])

def convolve(padded, weights, size_x, size_y, size_z):
    total = jnp.zeros((size_x * size_y * size_z, weights.shape[2]), jnp.float32)
    for tap in range(27):
        window = windowed(padded, tap, size_x, size_y, size_z)
        total = total + jnp.dot(window, weights[tap], preferred_element_type=jnp.float32)
    return total

def weight_grad(padded, grad, size_x, size_y, size_z):
    pieces = []
    for tap in range(27):
        window = windowed(padded, tap, size_x, size_y, size_z)
        pieces.append(jnp.dot(window.T, grad, preferred_element_type=jnp.float32))
    return jnp.stack(pieces, axis=0)

def pad_field(field):
    return jnp.pad(field, ((1, 1), (1, 1), (1, 1), (0, 0)))

def normalized(grad):
    return grad * lax.rsqrt(jnp.mean(grad * grad) + 1e-06)

def reference(volume, basin_mask, w_first, b_first, w_second, b_second, upstream):
    field = volume.reshape(NX, NY, NZ, CIN)
    active = basin_mask.astype(jnp.float32).reshape(-1, 1)
    padded_in = pad_field(field)
    pre_first = convolve(padded_in, w_first, NX, NY, NZ) + b_first
    sig_first = jax.nn.sigmoid(pre_first)
    hidden = (pre_first * sig_first * active).astype(jnp.bfloat16)
    padded_hidden = pad_field(hidden.reshape(NX, NY, NZ, COUT))
    pre_second = convolve(padded_hidden, w_second, NX, NY, NZ) + b_second
    sig_second = jax.nn.sigmoid(pre_second)
    features = (pre_second * sig_second * active).astype(jnp.bfloat16).reshape(NX, NY, NZ, COUT)
    grad_second = (upstream.reshape(-1, COUT).astype(jnp.float32) * active * sig_second * (1.0 + pre_second * (1.0 - sig_second))).astype(jnp.bfloat16)
    dw_second = weight_grad(padded_hidden, grad_second, NX, NY, NZ)
    flipped = jnp.transpose(w_second[::-1], (0, 2, 1))
    padded_grad = pad_field(grad_second.reshape(NX, NY, NZ, COUT))
    back_hidden = convolve(padded_grad, flipped, NX, NY, NZ)
    grad_first = (back_hidden * active * sig_first * (1.0 + pre_first * (1.0 - sig_first))).astype(jnp.bfloat16)
    dw_first = weight_grad(padded_in, grad_first, NX, NY, NZ)
    return (features, normalized(dw_first), normalized(dw_second))
```

```python
import jax
import jax.numpy as jnp
from jax import lax
from jax.sharding import PartitionSpec as P


def extended_2(block, sides, width):
    for axis, dim in sides:
        count = lax.axis_size(axis)
        forward = [(i, i + 1) for i in range(count - 1)]
        backward = [(target, source) for source, target in forward]
        low = lax.ppermute(
            lax.slice_in_dim(block, block.shape[dim] - width, None, axis=dim), axis, forward
        )
        high = lax.ppermute(lax.slice_in_dim(block, 0, width, axis=dim), axis, backward)
        block = jnp.concatenate([low, block, high], axis=dim)
    return block


def pad_depth(extended):
    return jnp.pad(extended, ((0, 0), (0, 0), (1, 1), (0, 0)))


def group_window(padded, tap_x, tap_y, cells_x, cells_y, cells_z):
    parts = [
        padded[tap_x : tap_x + cells_x, tap_y : tap_y + cells_y, tap_z : tap_z + cells_z]
        for tap_z in range(3)
    ]
    joined = jnp.concatenate(parts, axis=-1)
    return joined.reshape(cells_x * cells_y * cells_z, joined.shape[3])


def convolve(padded, weights, cells_x, cells_y, cells_z):
    chan_in = weights.shape[1]
    total = jnp.zeros((cells_x * cells_y * cells_z, weights.shape[2]), jnp.float32)
    for tap_x in range(3):
        for tap_y in range(3):
            window = group_window(padded, tap_x, tap_y, cells_x, cells_y, cells_z)
            first = 9 * tap_x + 3 * tap_y
            kernel = weights[first : first + 3].reshape(3 * chan_in, weights.shape[2])
            total = total + jnp.dot(window, kernel, preferred_element_type=jnp.float32)
    return total


def weight_grad(padded, grad, cells_x, cells_y, cells_z):
    pieces = []
    for tap_x in range(3):
        for tap_y in range(3):
            window = group_window(padded, tap_x, tap_y, cells_x, cells_y, cells_z)
            product = lax.dot_general(
                window, grad, (((0,), (0,)), ((), ())), preferred_element_type=jnp.float32
            )
            pieces.append(product.reshape(3, padded.shape[3], grad.shape[1]))
    return jnp.concatenate(pieces, axis=0)


def bit_levels(axes):
    levels = []
    for axis in axes:
        size = lax.axis_size(axis)
        bit = 1
        while bit < size:
            levels.append((axis, bit))
            bit *= 2
    return levels


def swap_with(part, axis, bit):
    return lax.ppermute(part, axis, [(i, i ^ bit) for i in range(lax.axis_size(axis))])


def side_of(axis, bit):
    return lax.rem(lax.axis_index(axis) // bit, 2)


def halves_summed(part, levels):
    for axis, bit in levels:
        half = part.shape[0] // 2
        side = side_of(axis, bit)
        sent = lax.dynamic_slice_in_dim(part, (1 - side) * half, half, 0).astype(jnp.bfloat16)
        kept = lax.dynamic_slice_in_dim(part, side * half, half, 0)
        part = kept + swap_with(sent, axis, bit).astype(jnp.float32)
    return part


def halves_joined(part, levels):
    for axis, bit in reversed(levels):
        other = swap_with(part, axis, bit)
        part = jnp.where(
            side_of(axis, bit) == 0,
            jnp.concatenate([part, other], axis=0),
            jnp.concatenate([other, part], axis=0),
        )
    return part


def summed_everywhere(rows, axes):
    levels = bit_levels(axes)
    pieces = 2 ** len(levels)
    padded = jnp.pad(rows, ((0, -rows.shape[0] % pieces), (0, 0)))
    summed = halves_summed(padded, levels).astype(jnp.bfloat16)
    return halves_joined(summed, levels)[: rows.shape[0]].astype(jnp.float32)


def normalized_with(grad, total, count):
    return grad * lax.rsqrt(total / count + 1e-06)


def on_device(volume, basin_mask, w_first, b_first, w_second, b_second, upstream):
    cells_x, cells_y, half_z, doubled = volume.shape
    chan_in = doubled // 2
    cells_z = 2 * half_z
    chan_out = w_first.shape[2]
    field = volume.reshape(cells_x, cells_y, cells_z, chan_in)
    active = basin_mask.astype(jnp.float32).reshape(-1, 1)
    padded_in = pad_depth(extended_2(field, (("gx", 0), ("gy", 1)), 1))
    pre_first = convolve(padded_in, w_first, cells_x, cells_y, cells_z) + b_first
    sig_first = jax.nn.sigmoid(pre_first)
    hidden = (
        (pre_first * sig_first * active)
        .astype(jnp.bfloat16)
        .reshape(cells_x, cells_y, cells_z, chan_out)
    )
    padded_hidden = pad_depth(extended_2(hidden, (("gx", 0), ("gy", 1)), 1))
    pre_second = convolve(padded_hidden, w_second, cells_x, cells_y, cells_z) + b_second
    sig_second = jax.nn.sigmoid(pre_second)
    features = (
        (pre_second * sig_second * active)
        .astype(jnp.bfloat16)
        .reshape(cells_x, cells_y, cells_z, chan_out)
    )
    grad_second = (
        upstream.reshape(-1, chan_out).astype(jnp.float32)
        * active
        * sig_second
        * (1.0 + pre_second * (1.0 - sig_second))
    ).astype(jnp.bfloat16)
    dw_second = weight_grad(padded_hidden, grad_second, cells_x, cells_y, cells_z)
    flipped = jnp.transpose(w_second[::-1], (0, 2, 1))
    grad_field = grad_second.reshape(cells_x, cells_y, cells_z, chan_out)
    padded_grad = pad_depth(extended_2(grad_field, (("gx", 0), ("gy", 1)), 1))
    back_hidden = convolve(padded_grad, flipped, cells_x, cells_y, cells_z)
    grad_first = (back_hidden * active * sig_first * (1.0 + pre_first * (1.0 - sig_first))).astype(
        jnp.bfloat16
    )
    dw_first = weight_grad(padded_in, grad_first, cells_x, cells_y, cells_z)
    count_first = float(dw_first.size)
    count_second = float(dw_second.size)
    rows_first = dw_first.shape[0] * dw_first.shape[1]
    rows = jnp.concatenate([dw_first.reshape(-1, chan_out), dw_second.reshape(-1, chan_out)], axis=0)
    sums = summed_everywhere(rows, ("gx", "gy"))
    sum_first = sums[:rows_first].reshape(dw_first.shape)
    sum_second = sums[rows_first:].reshape(dw_second.shape)
    step_first = normalized_with(sum_first, jnp.sum(sum_first * sum_first), count_first)
    step_second = normalized_with(sum_second, jnp.sum(sum_second * sum_second), count_second)
    return (features, step_first, step_second)


def solution(mesh):
    in_specs = (
        P("gx", "gy", None, None),
        P("gx", "gy", None),
        P(),
        P(),
        P(),
        P(),
        P("gx", "gy", None, None),
    )
    out_specs = (P("gx", "gy", None, None), P(), P())
    return jax.shard_map(
        on_device, mesh=mesh, in_specs=in_specs, out_specs=out_specs, check_vma=False
    )
```

```python
import functools

import jax
import jax.numpy as jnp
from jax import lax
from jax.experimental import pallas as pl
from jax.experimental.pallas import tpu as pltpu
from jax.sharding import PartitionSpec as P

BF = jnp.bfloat16
F32 = jnp.float32
LANES = 128
FIELD_HALO = 3
MASK_HALO = 2


def bit_levels(axes):
    levels = []
    for axis in axes:
        bit = 1
        while bit < lax.axis_size(axis):
            levels.append((axis, bit))
            bit *= 2
    return levels


def swap_with(part, axis, bit):
    return lax.ppermute(part, axis, [(i, i ^ bit) for i in range(lax.axis_size(axis))])


def side_of(axis, bit):
    return lax.rem(lax.axis_index(axis) // bit, 2)


def halves_summed(part, levels):
    for axis, bit in levels:
        half = part.shape[0] // 2
        side = side_of(axis, bit)
        sent = lax.dynamic_slice_in_dim(part, (1 - side) * half, half, 0).astype(BF)
        kept = lax.dynamic_slice_in_dim(part, side * half, half, 0)
        part = kept + swap_with(sent, axis, bit).astype(F32)
    return part


def halves_joined(part, levels):
    for axis, bit in reversed(levels):
        other = swap_with(part, axis, bit)
        part = jnp.where(
            side_of(axis, bit) == 0,
            jnp.concatenate([part, other], axis=0),
            jnp.concatenate([other, part], axis=0),
        )
    return part


def summed_everywhere(rows, axes):
    levels = bit_levels(axes)
    pieces = 2 ** len(levels)
    padded = jnp.pad(rows, ((0, -rows.shape[0] % pieces), (0, 0)))
    summed = halves_summed(padded, levels).astype(BF)
    return halves_joined(summed, levels)[: rows.shape[0]].astype(F32)


def normalized_with(grad, total, count):
    return grad * lax.rsqrt(total / count + 1e-06)


def exchange(forward, backward, axis):
    count = lax.axis_size(axis)
    ups = [(i, i + 1) for i in range(count - 1)]
    downs = [(target, source) for source, target in ups]
    return lax.ppermute(forward, axis, ups), lax.ppermute(backward, axis, downs)


def pack_x_body(cx, field, up, tile, last, first):
    for ref, at_field, at_up in ((last, cx - FIELD_HALO, cx - 1), (first, 0, 0)):
        rows = field[at_field : at_field + FIELD_HALO].reshape(-1, LANES)
        ups = up[at_up : at_up + 1].reshape(-1, LANES)
        ref[0 : rows.shape[0]] = rows
        ref[rows.shape[0] : rows.shape[0] + ups.shape[0]] = ups
        ref[rows.shape[0] + ups.shape[0] :] = tile[...]


def pack_y_body(cx, cy, kz, field, up, tile, low, high, last, first):
    nf = FIELD_HALO * cy * kz
    nu = cy * 2 * kz
    for ref, at_field, at_up in ((last, cy - FIELD_HALO, cy - 1), (first, 0, 0)):
        row = 0
        ends = [m[0:nf].reshape(FIELD_HALO, cy, kz, LANES) for m in (low, high)]
        for part in (ends[0], field, ends[1]):
            rows = part[:, at_field : at_field + FIELD_HALO].reshape(-1, LANES)
            ref[row : row + rows.shape[0]] = rows
            row += rows.shape[0]
        ends = [m[nf : nf + nu].reshape(1, cy, 2 * kz, LANES) for m in (low, high)]
        for part in (ends[0], up, ends[1]):
            rows = part[:, at_up : at_up + 1].reshape(-1, LANES)
            ref[row : row + rows.shape[0]] = rows
            row += rows.shape[0]
        for part in (low[nf + nu :], tile[...], high[nf + nu :]):
            ref[row : row + kz] = part
            row += kz


def side_pair(pair, kz, width):
    rows = pair.shape[0]
    depth = lax.rem(lax.broadcasted_iota(jnp.int32, (rows, width), 0), kz)
    above = pltpu.roll(pair[:, :width], rows - 1, 0)
    below = pltpu.roll(pair[:, width:], 1, 0)
    above = jnp.where(depth == kz - 1, 0.0, above)
    below = jnp.where(depth == 0, 0.0, below)
    return above, below


def taps_of(pair, side, at, rows, cols):
    parts = []
    for a in range(3):
        for b in range(3):
            for ref in (pair, side):
                part = ref[pl.ds(at + a, rows), b : b + cols]
                parts.append(part.reshape(-1, part.shape[-1]))
    return jnp.concatenate(parts, axis=1)


def forward_body(
    cx, cy, kz,
    field, up, tile, low, high, left, right, w1, b1, w2, b2,
    features, d2, g2p, g2s, gate, xp, xs,
    hp, hs, act, upf, outf,
):
    fh, mh = FIELD_HALO, MASK_HALO
    nf, nu = fh * cy * kz, cy * 2 * kz
    ex = cx + 2 * fh
    xp[fh : fh + cx, fh : fh + cy] = field[...]
    xp[0:fh, fh : fh + cy] = low[0:nf].reshape(fh, cy, kz, LANES)
    xp[fh + cx :, fh : fh + cy] = high[0:nf].reshape(fh, cy, kz, LANES)
    ne = ex * fh * kz
    xp[:, 0:fh] = left[0:ne].reshape(ex, fh, kz, LANES)
    xp[:, fh + cy :] = right[0:ne].reshape(ex, fh, kz, LANES)
    ey = cy + 2 * fh

    def fill_side(i, carry):
        rows = xp[i].reshape(ey * kz, LANES).astype(F32)
        depth = lax.rem(lax.broadcasted_iota(jnp.int32, rows.shape, 0), kz)
        lane = lax.broadcasted_iota(jnp.int32, rows.shape, 1)
        above = jnp.where(depth == kz - 1, 0.0, pltpu.roll(rows, ey * kz - 1, 0))
        below = jnp.where(depth == 0, 0.0, pltpu.roll(rows, 1, 0))
        both = jnp.where(lane < LANES // 2, above, below).astype(BF)
        xs[i] = both.reshape(ey, kz, LANES)
        return carry

    lax.fori_loop(0, ex, fill_side, 0)
    uy = cy + 2
    span = uy * 2 * kz

    def put_up(x, y, cols, value):
        base = x * span + y * 2 * kz
        upf[base : base + cols * 2 * kz] = value.reshape(-1, LANES).astype(F32)

    for x in range(cx):
        put_up(x + 1, 1, cy, up[x])
    put_up(0, 1, cy, low[nf : nf + nu])
    put_up(cx + 1, 1, cy, high[nf : nf + nu])
    for x in range(cx + 2):
        at = ne + x * 2 * kz
        put_up(x, 0, 1, left[at : at + 2 * kz])
        put_up(x, cy + 1, 1, right[at : at + 2 * kz])
    nm = ne + (cx + 2) * 2 * kz

    def put_mask(source, sx, sy, x, y):
        lane = 2 * (sx * cy + sy)
        for parity in range(2):
            value = jnp.broadcast_to(source[:, lane + parity : lane + parity + 1], (kz, LANES))
            act[x, y, :, parity * LANES : (parity + 1) * LANES] = value.astype(BF)

    def row_tiles(ref, start):
        own = [(ref[start + i * kz : start + (i + 1) * kz].astype(F32)) for i in range(3)]
        rows = []
        for x in range(cx + 2 * mh):
            if x < mh:
                rows.append((own[0], cx - mh + x))
            elif x < mh + cx:
                rows.append((own[1], x - mh))
            else:
                rows.append((own[2], x - mh - cx))
        return rows

    mid = tile[...].astype(F32)
    lo_tile = low[nf + nu : nf + nu + kz].astype(F32)
    hi_tile = high[nf + nu : nf + nu + kz].astype(F32)
    left_rows, right_rows = row_tiles(left, nm), row_tiles(right, nm)
    for x in range(cx + 2 * mh):
        if x < mh:
            source, sx = lo_tile, cx - mh + x
        elif x < mh + cx:
            source, sx = mid, x - mh
        else:
            source, sx = hi_tile, x - mh - cx
        for y in range(cy):
            put_mask(source, sx, y, x, mh + y)
        for j in range(mh):
            put_mask(*left_rows[x], cy - mh + j, x, j)
            put_mask(*right_rows[x], j, x, mh + cy + j)

    hx, hy = cx + 4, cy + 4
    step = 2

    def first(i, carry):
        at = i * step
        window = taps_of(xp, xs, at, step, hy)
        z = jnp.dot(window, w1[...], preferred_element_type=F32) + b1[...]
        s = jax.nn.sigmoid(z)
        m = act[pl.ds(at, step)].reshape(step * hy * kz, 2 * LANES).astype(F32)
        h = z * s * m
        above, below = side_pair(h, kz, LANES)
        hp[pl.ds(at, step)] = h.astype(BF).reshape(step, hy, kz, 2 * LANES)
        both = jnp.concatenate([above, below], axis=1).astype(BF)
        hs[pl.ds(at, step)] = both.reshape(step, hy, kz, 2 * LANES)

        @pl.when(jnp.logical_and(i >= 2 // step, i < (2 + cx) // step))
        def _():
            factor = m * s * (1.0 + z * (1.0 - s))
            factor = factor.reshape(step, hy, kz, 2 * LANES)[:, 2 : 2 + cy]
            gate[pl.ds(at - 2, step)] = factor

        return carry

    lax.fori_loop(0, hx // step, first, 0)

    def second(i, carry):
        at = i * step
        window = taps_of(hp, hs, at, step, uy)
        z = jnp.dot(window, w2[...], preferred_element_type=F32) + b2[...]
        s = jax.nn.sigmoid(z)
        m = act[pl.ds(at + 1, step), 1 : 1 + uy].reshape(-1, 2 * LANES).astype(F32)
        rows = step * uy * kz
        base = pl.multiple_of(at * span, 8)
        u = jnp.concatenate(
            [upf[pl.ds(base, rows, stride=2), :], upf[pl.ds(base + 1, rows, stride=2), :]], axis=1
        )
        g = u * m * s * (1.0 + z * (1.0 - s))
        gb = g.astype(BF)
        above, below = side_pair(g, kz, LANES)
        g2p[pl.ds(at, step)] = gb.reshape(step, uy, kz, 2 * LANES)
        both = jnp.concatenate([above, below], axis=1).astype(BF)
        g2s[pl.ds(at, step)] = both.reshape(step, uy, kz, 2 * LANES)
        out = z * s * m
        outf[pl.ds(base, rows, stride=2), :] = out[:, :LANES]
        outf[pl.ds(base + 1, rows, stride=2), :] = out[:, LANES:]
        return carry

    lax.fori_loop(0, (cx + 2) // step, second, 0)
    for x in range(cx):
        base = (x + 1) * span + 2 * kz
        rows = outf[base : base + cy * 2 * kz].astype(BF)
        features[x] = rows.reshape(cy, 2 * kz, LANES)

    own = hp[2 : 2 + cx, 2 : 2 + cy].reshape(-1, 2 * LANES)
    turned = own.T
    for a in range(3):
        for b in range(3):
            parts = [
                ref[2 - a : 2 - a + cx, 2 - b : 2 - b + cy].reshape(-1, 2 * LANES)
                for ref in (g2p, g2s)
            ]
            for half, part in enumerate(parts):
                block = jnp.dot(turned, part, preferred_element_type=F32)
                q = [[block[r * LANES : (r + 1) * LANES, c * LANES : (c + 1) * LANES] for c in (0, 1)] for r in (0, 1)]
                t = 9 * a + 3 * b
                if half == 0:
                    d2[t + 1] = q[0][0] + q[1][1]
                    d2[t] = q[0][1]
                    d2[t + 2] = q[1][0]
                else:
                    d2[t] = d2[t] + q[1][0]
                    d2[t + 2] = d2[t + 2] + q[0][1]


def backward_body(cx, cy, kz, g2p, g2s, gate, xp, xs, w3, d1, g1):
    fh = FIELD_HALO
    step = 2
    rows = step * cy * kz

    def grad(i, carry):
        at = i * step
        window = taps_of(g2p, g2s, at, step, cy)
        e = jnp.dot(window, w3[...], preferred_element_type=F32)
        g = e * gate[pl.ds(at, step)].reshape(rows, 2 * LANES)
        g1[pl.ds(pl.multiple_of(i * rows, rows), rows)] = g.astype(BF)
        return carry

    lax.fori_loop(0, cx // step, grad, 0)
    right = g1[...]
    cells = cx * cy * kz
    half = LANES // 2
    for b in range(3):
        cols = slice(fh - 1 + b, fh - 1 + b + cy)
        parts = [ref[fh - 1 : fh + 1 + cx, cols].reshape(-1, LANES) for ref in (xp, xs)]
        turned = jnp.concatenate(parts, axis=1).T
        for a in range(3):
            at = a * cy * kz
            block = jnp.dot(turned[:, at : at + cells], right, preferred_element_type=F32)
            q = [
                [block[r * half : (r + 1) * half, c * LANES : (c + 1) * LANES] for c in (0, 1)]
                for r in range(4)
            ]
            t = 9 * a + 3 * b
            d1[t] = q[0][1] + q[3][0]
            d1[t + 1] = q[0][0] + q[1][1]
            d1[t + 2] = q[1][0] + q[2][1]


def pair_weights(w):
    w = w.reshape(9, 3, w.shape[1], w.shape[2])
    none = jnp.zeros_like(w[:, 0])
    even = jnp.concatenate([w[:, 1], w[:, 2], none, w[:, 0]], axis=1)
    odd = jnp.concatenate([w[:, 0], w[:, 1], w[:, 2], none], axis=1)
    both = jnp.concatenate([even, odd], axis=2)
    return both.reshape(-1, both.shape[2])


def on_device(volume, basin_mask, w_first, b_first, w_second, b_second, upstream):
    cx, cy, kz, _ = volume.shape
    chan = w_first.shape[2]
    tile = basin_mask.astype(BF).reshape(cx * cy, kz, 2).transpose(1, 0, 2)
    tile = tile.reshape(kz, 2 * cx * cy)
    tile = jnp.pad(tile, ((0, 0), (0, LANES - tile.shape[1])))
    shape = jax.ShapeDtypeStruct
    rows_x = FIELD_HALO * cy * kz + cy * 2 * kz + kz
    last, first = pl.pallas_call(
        functools.partial(pack_x_body, cx),
        out_shape=[shape((rows_x, LANES), BF)] * 2,
        name="pack_x",
    )(volume, upstream, tile)
    low, high = exchange(last, first, "gx")
    rows_y = (cx + 2 * FIELD_HALO) * FIELD_HALO * kz + (cx + 2) * 2 * kz + 3 * kz
    last, first = pl.pallas_call(
        functools.partial(pack_y_body, cx, cy, kz),
        out_shape=[shape((rows_y, LANES), BF)] * 2,
        name="pack_y",
    )(volume, upstream, tile, low, high)
    left, right = exchange(last, first, "gy")
    w1, w2 = pair_weights(w_first), pair_weights(w_second)
    w3 = pair_weights(jnp.transpose(w_second[::-1], (0, 2, 1)))
    b1 = jnp.concatenate([b_first, b_first]).reshape(1, -1)
    b2 = jnp.concatenate([b_second, b_second]).reshape(1, -1)
    ex, ey = cx + 2 * FIELD_HALO, cy + 2 * FIELD_HALO
    features, d2, g2p, g2s, gate, xp, xs = pl.pallas_call(
        functools.partial(forward_body, cx, cy, kz),
        out_shape=[
            shape((cx, cy, 2 * kz, chan), BF),
            shape(w_second.shape, F32),
            shape((cx + 2, cy + 2, kz, 2 * chan), BF),
            shape((cx + 2, cy + 2, kz, 2 * chan), BF),
            shape((cx, cy, kz, 2 * chan), F32),
            shape((ex, ey, kz, LANES), BF),
            shape((ex, ey, kz, LANES), BF),
        ],
        scratch_shapes=[
            pltpu.VMEM((cx + 4, cy + 4, kz, 2 * chan), BF),
            pltpu.VMEM((cx + 4, cy + 4, kz, 2 * chan), BF),
            pltpu.VMEM((cx + 4, cy + 4, kz, 2 * chan), BF),
            pltpu.VMEM(((cx + 2) * (cy + 2) * 2 * kz, LANES), F32),
            pltpu.VMEM(((cx + 2) * (cy + 2) * 2 * kz, LANES), F32),
        ],
        name="forward",
    )(volume, upstream, tile, low, high, left, right, w1, b1, w2, b2)
    d1 = pl.pallas_call(
        functools.partial(backward_body, cx, cy, kz),
        out_shape=shape(w_first.shape, F32),
        scratch_shapes=[pltpu.VMEM((cx * cy * kz, 2 * chan), BF)],
        name="backward",
    )(g2p, g2s, gate, xp, xs, w3)
    rows_first = d1.shape[0] * d1.shape[1]
    rows = jnp.concatenate([d1.reshape(-1, chan), d2.reshape(-1, chan)], axis=0)
    sums = summed_everywhere(rows, ("gx", "gy"))
    sum_first = sums[:rows_first].reshape(d1.shape)
    sum_second = sums[rows_first:].reshape(d2.shape)
    step_first = normalized_with(sum_first, jnp.sum(sum_first * sum_first), float(d1.size))
    step_second = normalized_with(sum_second, jnp.sum(sum_second * sum_second), float(d2.size))
    return (features, step_first, step_second)


def solution(mesh):
    in_specs = (
        P("gx", "gy", None, None),
        P("gx", "gy", None),
        P(),
        P(),
        P(),
        P(),
        P("gx", "gy", None, None),
    )
    out_specs = (P("gx", "gy", None, None), P(), P())
    return jax.shard_map(
        on_device, mesh=mesh, in_specs=in_specs, out_specs=out_specs, check_vma=False
    )
```

```python
import functools

import jax
import jax.numpy as jnp
from jax import lax
from jax.experimental import pallas as pl
from jax.experimental.pallas import tpu as pltpu
from jax.sharding import PartitionSpec as P

BF = jnp.bfloat16
F32 = jnp.float32
LANES = 128
FIELD_HALO = 3
MASK_HALO = 2


def bit_levels(axes):
    levels = []
    for axis in axes:
        bit = 1
        while bit < lax.axis_size(axis):
            levels.append((axis, bit))
            bit *= 2
    return levels


def swap(part, level):
    axis, bit = level
    return lax.ppermute(part, axis, [(i, i ^ bit) for i in range(lax.axis_size(axis))])


def side_of(level):
    axis, bit = level
    return lax.rem(lax.axis_index(axis) // bit, 2)


def halves(part, level):
    half = part.shape[1] // 2
    side = side_of(level)
    sent = lax.dynamic_slice_in_dim(part, (1 - side) * half, half, 1).astype(BF)
    kept = lax.dynamic_slice_in_dim(part, side * half, half, 1)
    return sent, kept


def joined(own, other, level):
    return jnp.where(
        side_of(level) == 0,
        jnp.concatenate([own, other], axis=1),
        jnp.concatenate([other, own], axis=1),
    )


def summed_inner(second, first, levels):
    middle, final = levels[:-1], levels[-1]
    for level in middle:
        sent2, kept2 = halves(second, level)
        sent1, kept1 = halves(first, level)
        cut = sent2.shape[1]
        got = swap(jnp.concatenate([sent2, sent1], axis=1), level).astype(F32)
        second, first = kept2 + got[:, :cut], kept1 + got[:, cut:]
    cut = second.shape[1]
    both = jnp.concatenate([second, first], axis=1).astype(BF)
    both = (both.astype(F32) + swap(both, final).astype(F32)).astype(BF)
    for level in reversed(middle):
        got = swap(both, level)
        both = jnp.concatenate(
            [joined(both[:, :cut], got[:, :cut], level), joined(both[:, cut:], got[:, cut:], level)],
            axis=1,
        )
        cut *= 2
    return both[:, :cut], both[:, cut:]


def exchange(forward, backward, axis):
    count = lax.axis_size(axis)
    ups = [(i, i + 1) for i in range(count - 1)]
    downs = [(target, source) for source, target in ups]
    return lax.ppermute(forward, axis, ups), lax.ppermute(backward, axis, downs)


def pack_x_body(cx, cy, kz, field, up, mask, last, first, tile, square, deep):
    cells = cx * cy
    square[...] = jnp.zeros_like(square)
    square[0:cells, 0 : 2 * kz] = mask[...].reshape(cells, 2 * kz).astype(F32)
    deep[...] = square[...].T
    even = deep[pl.ds(0, kz, stride=2), :]
    odd = deep[pl.ds(1, kz, stride=2), :]
    tile[...] = (even + pltpu.roll(odd, LANES // 2, 1)).astype(BF)
    for ref, at_field, at_up in ((last, cx - FIELD_HALO, cx - 1), (first, 0, 0)):
        rows = field[at_field : at_field + FIELD_HALO].reshape(-1, LANES)
        ups = up[at_up : at_up + 1].reshape(-1, LANES)
        ref[0 : rows.shape[0]] = rows
        ref[rows.shape[0] : rows.shape[0] + ups.shape[0]] = ups
        ref[rows.shape[0] + ups.shape[0] :] = tile[...]


def pack_y_body(cx, cy, kz, field, up, tile, low, high, last, first):
    nf = FIELD_HALO * cy * kz
    nu = cy * 2 * kz
    for ref, at_field, at_up in ((last, cy - FIELD_HALO, cy - 1), (first, 0, 0)):
        row = 0
        ends = [m[0:nf].reshape(FIELD_HALO, cy, kz, LANES) for m in (low, high)]
        for part in (ends[0], field, ends[1]):
            rows = part[:, at_field : at_field + FIELD_HALO].reshape(-1, LANES)
            ref[row : row + rows.shape[0]] = rows
            row += rows.shape[0]
        ends = [m[nf : nf + nu].reshape(1, cy, 2 * kz, LANES) for m in (low, high)]
        for part in (ends[0], up, ends[1]):
            rows = part[:, at_up : at_up + 1].reshape(-1, LANES)
            ref[row : row + rows.shape[0]] = rows
            row += rows.shape[0]
        for part in (low[nf + nu :], tile[...], high[nf + nu :]):
            ref[row : row + kz] = part
            row += kz


def side_pair(pair, kz, width):
    rows = pair.shape[0]
    depth = lax.rem(lax.broadcasted_iota(jnp.int32, (rows, width), 0), kz)
    above = pltpu.roll(pair[:, :width], rows - 1, 0)
    below = pltpu.roll(pair[:, width:], 1, 0)
    above = jnp.where(depth == kz - 1, 0.0, above)
    below = jnp.where(depth == 0, 0.0, below)
    return above, below


def taps_of(pair, side, at, rows, cols):
    parts = []
    for a in range(3):
        for b in range(3):
            for ref in (pair, side):
                part = ref[pl.ds(at + a, rows), b : b + cols]
                parts.append(part.reshape(-1, part.shape[-1]))
    return jnp.concatenate(parts, axis=1)


def forward_body(
    cx, cy, kz,
    side, field, up, tile, low, high, left, right, w1, b1, w2, b2,
    features, sent, kept, g2p, g2s, gate, xp, xs,
    hp, hs, act, upf, outf, d2,
):
    fh, mh = FIELD_HALO, MASK_HALO
    nf, nu = fh * cy * kz, cy * 2 * kz
    ex = cx + 2 * fh
    xp[fh : fh + cx, fh : fh + cy] = field[...]
    xp[0:fh, fh : fh + cy] = low[0:nf].reshape(fh, cy, kz, LANES)
    xp[fh + cx :, fh : fh + cy] = high[0:nf].reshape(fh, cy, kz, LANES)
    ne = ex * fh * kz
    xp[:, 0:fh] = left[0:ne].reshape(ex, fh, kz, LANES)
    xp[:, fh + cy :] = right[0:ne].reshape(ex, fh, kz, LANES)
    ey = cy + 2 * fh

    def fill_side(i, carry):
        rows = xp[i].reshape(ey * kz, LANES).astype(F32)
        depth = lax.rem(lax.broadcasted_iota(jnp.int32, rows.shape, 0), kz)
        lane = lax.broadcasted_iota(jnp.int32, rows.shape, 1)
        above = jnp.where(depth == kz - 1, 0.0, pltpu.roll(rows, ey * kz - 1, 0))
        below = jnp.where(depth == 0, 0.0, pltpu.roll(rows, 1, 0))
        both = jnp.where(lane < LANES // 2, above, below).astype(BF)
        xs[i] = both.reshape(ey, kz, LANES)
        return carry

    lax.fori_loop(0, ex, fill_side, 0)
    uy = cy + 2
    span = uy * 2 * kz

    def put_up(x, y, cols, value):
        base = x * span + y * 2 * kz
        upf[base : base + cols * 2 * kz] = value.reshape(-1, LANES).astype(F32)

    for x in range(cx):
        put_up(x + 1, 1, cy, up[x])
    put_up(0, 1, cy, low[nf : nf + nu])
    put_up(cx + 1, 1, cy, high[nf : nf + nu])
    for x in range(cx + 2):
        at = ne + x * 2 * kz
        put_up(x, 0, 1, left[at : at + 2 * kz])
        put_up(x, cy + 1, 1, right[at : at + 2 * kz])
    nm = ne + (cx + 2) * 2 * kz

    def put_mask(source, sx, sy, x, y):
        for parity in range(2):
            lane = sx * cy + sy + parity * (LANES // 2)
            value = jnp.broadcast_to(source[:, lane : lane + 1], (kz, LANES))
            act[x, y, :, parity * LANES : (parity + 1) * LANES] = value.astype(BF)

    def row_tiles(ref, start):
        own = [(ref[start + i * kz : start + (i + 1) * kz].astype(F32)) for i in range(3)]
        rows = []
        for x in range(cx + 2 * mh):
            if x < mh:
                rows.append((own[0], cx - mh + x))
            elif x < mh + cx:
                rows.append((own[1], x - mh))
            else:
                rows.append((own[2], x - mh - cx))
        return rows

    mid = tile[...].astype(F32)
    lo_tile = low[nf + nu : nf + nu + kz].astype(F32)
    hi_tile = high[nf + nu : nf + nu + kz].astype(F32)
    left_rows, right_rows = row_tiles(left, nm), row_tiles(right, nm)
    for x in range(cx + 2 * mh):
        if x < mh:
            source, sx = lo_tile, cx - mh + x
        elif x < mh + cx:
            source, sx = mid, x - mh
        else:
            source, sx = hi_tile, x - mh - cx
        for y in range(cy):
            put_mask(source, sx, y, x, mh + y)
        for j in range(mh):
            put_mask(*left_rows[x], cy - mh + j, x, j)
            put_mask(*right_rows[x], j, x, mh + cy + j)

    hx, hy = cx + 4, cy + 4
    step = 2

    def first(i, carry):
        at = i * step
        window = taps_of(xp, xs, at, step, hy)
        z = jnp.dot(window, w1[...], preferred_element_type=F32) + b1[...]
        s = jax.nn.sigmoid(z)
        m = act[pl.ds(at, step)].reshape(step * hy * kz, 2 * LANES).astype(F32)
        h = z * s * m
        above, below = side_pair(h, kz, LANES)
        hp[pl.ds(at, step)] = h.astype(BF).reshape(step, hy, kz, 2 * LANES)
        both = jnp.concatenate([above, below], axis=1).astype(BF)
        hs[pl.ds(at, step)] = both.reshape(step, hy, kz, 2 * LANES)

        @pl.when(jnp.logical_and(i >= 2 // step, i < (2 + cx) // step))
        def _():
            factor = m * s * (1.0 + z * (1.0 - s))
            factor = factor.reshape(step, hy, kz, 2 * LANES)[:, 2 : 2 + cy]
            gate[pl.ds(at - 2, step)] = factor

        return carry

    lax.fori_loop(0, hx // step, first, 0)

    def second(i, carry):
        at = i * step
        window = taps_of(hp, hs, at, step, uy)
        z = jnp.dot(window, w2[...], preferred_element_type=F32) + b2[...]
        s = jax.nn.sigmoid(z)
        m = act[pl.ds(at + 1, step), 1 : 1 + uy].reshape(-1, 2 * LANES).astype(F32)
        rows = step * uy * kz
        base = pl.multiple_of(at * span, 8)
        u = jnp.concatenate(
            [upf[pl.ds(base, rows, stride=2), :], upf[pl.ds(base + 1, rows, stride=2), :]], axis=1
        )
        g = u * m * s * (1.0 + z * (1.0 - s))
        gb = g.astype(BF)
        above, below = side_pair(g, kz, LANES)
        g2p[pl.ds(at, step)] = gb.reshape(step, uy, kz, 2 * LANES)
        both = jnp.concatenate([above, below], axis=1).astype(BF)
        g2s[pl.ds(at, step)] = both.reshape(step, uy, kz, 2 * LANES)
        out = z * s * m
        outf[pl.ds(base, rows, stride=2), :] = out[:, :LANES]
        outf[pl.ds(base + 1, rows, stride=2), :] = out[:, LANES:]
        return carry

    lax.fori_loop(0, (cx + 2) // step, second, 0)
    for x in range(cx):
        base = (x + 1) * span + 2 * kz
        rows = outf[base : base + cy * 2 * kz].astype(BF)
        features[x] = rows.reshape(cy, 2 * kz, LANES)

    own = hp[2 : 2 + cx, 2 : 2 + cy].reshape(-1, 2 * LANES)
    turned = own.T
    for a in range(3):
        for b in range(3):
            parts = [
                ref[2 - a : 2 - a + cx, 2 - b : 2 - b + cy].reshape(-1, 2 * LANES)
                for ref in (g2p, g2s)
            ]
            for half, part in enumerate(parts):
                block = jnp.dot(turned, part, preferred_element_type=F32)
                q = [[block[r * LANES : (r + 1) * LANES, c * LANES : (c + 1) * LANES] for c in (0, 1)] for r in (0, 1)]
                t = 9 * a + 3 * b
                if half == 0:
                    d2[t + 1] = q[0][0] + q[1][1]
                    d2[t] = q[0][1]
                    d2[t + 2] = q[1][0]
                else:
                    d2[t] = d2[t] + q[1][0]
                    d2[t + 2] = d2[t + 2] + q[0][1]
    split_rows(side, d2, sent, kept)


def split_rows(side, total, sent, kept):
    half = total.shape[1] // 2
    mine = pl.multiple_of(side[0] * half, half)
    other = pl.multiple_of((1 - side[0]) * half, half)
    sent[...] = total[:, pl.ds(other, half)].astype(BF)
    kept[...] = total[:, pl.ds(mine, half)]


def grad_body(cx, cy, kz, g2p, g2s, gate, w3, g1):
    step = 2
    rows = step * cy * kz

    def grad(i, carry):
        at = i * step
        window = taps_of(g2p, g2s, at, step, cy)
        e = jnp.dot(window, w3[...], preferred_element_type=F32)
        g = e * gate[pl.ds(at, step)].reshape(rows, 2 * LANES)
        g1[pl.ds(pl.multiple_of(i * rows, rows), rows)] = g.astype(BF)
        return carry

    lax.fori_loop(0, cx // step, grad, 0)


def first_body(cx, cy, kz, side, xp, xs, g1, sent, kept, d1):
    fh = FIELD_HALO
    right = g1[...]
    cells = cx * cy * kz
    half = LANES // 2
    for b in range(3):
        cols = slice(fh - 1 + b, fh - 1 + b + cy)
        parts = [ref[fh - 1 : fh + 1 + cx, cols].reshape(-1, LANES) for ref in (xp, xs)]
        turned = jnp.concatenate(parts, axis=1).T
        for a in range(3):
            at = a * cy * kz
            block = jnp.dot(turned[:, at : at + cells], right, preferred_element_type=F32)
            q = [
                [block[r * half : (r + 1) * half, c * LANES : (c + 1) * LANES] for c in (0, 1)]
                for r in range(4)
            ]
            t = 9 * a + 3 * b
            d1[t] = q[0][1] + q[3][0]
            d1[t + 1] = q[0][0] + q[1][1]
            d1[t + 2] = q[1][0] + q[2][1]
    split_rows(side, d1, sent, kept)


def norm_body(side, own2, other2, own1, other1, out2, out1):
    for own, other, out in ((own2, other2, out2), (own1, other1, out1)):
        half = own.shape[1]
        mine, rest = own[...].astype(F32), other[...].astype(F32)
        total = jnp.sum(mine * mine) + jnp.sum(rest * rest)
        scale = lax.rsqrt(jnp.full((1, LANES), total) / float(out.size) + 1e-06)
        out[:, pl.ds(pl.multiple_of(side[0] * half, half), half)] = mine * scale
        out[:, pl.ds(pl.multiple_of((1 - side[0]) * half, half), half)] = rest * scale


PAIR_TAPS = ((1, 0), (2, 1), (None, 2), (0, None))


def weights_body(first, second, w1, w2, w3):
    taps = second.shape[0]

    def group(g, carry):
        for source, out, turn in ((first, w1, False), (second, w2, False), (second, w3, True)):
            depth, width = source.shape[1:]
            if turn:
                block = [source[taps - 1 - 3 * g - c].astype(F32).T.astype(BF) for c in range(3)]
            else:
                block = [source[3 * g + c] for c in range(3)]
            none = jnp.zeros((depth, width), BF)
            for r, row in enumerate(PAIR_TAPS):
                at = pl.multiple_of(g * 4 * depth + r * depth, depth)
                for c, tap in enumerate(row):
                    value = none if tap is None else block[tap]
                    out[pl.ds(at, depth), c * width : (c + 1) * width] = value
        return carry

    lax.fori_loop(0, taps // 3, group, 0)


def local_call(body, name, out, scratch=(), scalars=0, in_hbm=(), out_hbm=()):
    def call(*args):
        vmem = pl.BlockSpec(memory_space=pltpu.VMEM)
        plain = pl.BlockSpec()
        ins = [
            pl.BlockSpec(memory_space=pltpu.SMEM) if i < scalars else plain if i in in_hbm else vmem
            for i in range(len(args))
        ]
        return pl.pallas_call(
            body,
            out_shape=out,
            in_specs=ins,
            out_specs=[plain if i in out_hbm else vmem for i in range(len(out))],
            scratch_shapes=list(scratch),
            name=name,
        )(*args)

    return call


def on_device(volume, basin_mask, w_first, b_first, w_second, b_second, upstream):
    cx, cy, kz, _ = volume.shape
    taps, _, chan = w_first.shape
    part = functools.partial
    shape = jax.ShapeDtypeStruct
    levels = bit_levels(("gx", "gy"))
    core, one, two = levels[:3]
    side = side_of(core).astype(jnp.int32).reshape(1)
    rows_x = FIELD_HALO * cy * kz + cy * 2 * kz + kz
    last, first, tile = local_call(
        part(pack_x_body, cx, cy, kz),
        "pack_x",
        [shape((rows_x, LANES), BF)] * 2 + [shape((kz, LANES), BF)],
        [pltpu.VMEM((LANES, LANES), F32)] * 2,
    )(volume, upstream, basin_mask)
    low, high = exchange(last, first, "gx")
    w1, w2, w3 = local_call(
        weights_body,
        "weights",
        [
            shape((4 * taps // 3 * w_first.shape[1], 2 * chan), BF),
            shape((4 * taps // 3 * chan, 2 * chan), BF),
            shape((4 * taps // 3 * chan, 2 * chan), BF),
        ],
    )(w_first, w_second)
    rows_y = (cx + 2 * FIELD_HALO) * FIELD_HALO * kz + (cx + 2) * 2 * kz + 3 * kz
    last, first = local_call(
        part(pack_y_body, cx, cy, kz), "pack_y", [shape((rows_y, LANES), BF)] * 2
    )(volume, upstream, tile, low, high)
    left, right = exchange(last, first, "gy")
    b1 = jnp.concatenate([b_first, b_first]).reshape(1, -1)
    b2 = jnp.concatenate([b_second, b_second]).reshape(1, -1)
    ex, ey = cx + 2 * FIELD_HALO, cy + 2 * FIELD_HALO
    features, sent2, kept2, g2p, g2s, gate, xp, xs = local_call(
        part(forward_body, cx, cy, kz),
        "forward",
        [
            shape((cx, cy, 2 * kz, chan), BF),
            shape((taps, chan // 2, chan), BF),
            shape((taps, chan // 2, chan), F32),
            shape((cx + 2, cy + 2, kz, 2 * chan), BF),
            shape((cx + 2, cy + 2, kz, 2 * chan), BF),
            shape((cx, cy, kz, 2 * chan), F32),
            shape((ex, ey, kz, LANES), BF),
            shape((ex, ey, kz, LANES), BF),
        ],
        [
            pltpu.VMEM((cx + 4, cy + 4, kz, 2 * chan), BF),
            pltpu.VMEM((cx + 4, cy + 4, kz, 2 * chan), BF),
            pltpu.VMEM((cx + 4, cy + 4, kz, 2 * chan), BF),
            pltpu.VMEM(((cx + 2) * (cy + 2) * 2 * kz, LANES), F32),
            pltpu.VMEM(((cx + 2) * (cy + 2) * 2 * kz, LANES), F32),
            pltpu.VMEM(w_second.shape, F32),
        ],
        scalars=1,
    )(side, volume, upstream, tile, low, high, left, right, w1, b1, w2, b2)
    got2 = swap(sent2, core)
    (g1,) = local_call(
        part(grad_body, cx, cy, kz), "grad_first", [shape((cx * cy * kz, 2 * chan), BF)]
    )(g2p, g2s, gate, w3)
    sent2, kept2 = halves(kept2 + got2.astype(F32), one)
    sent2, g1 = lax.optimization_barrier((sent2, g1))
    got2 = swap(sent2, one)
    half = w_first.shape[1] // 2
    sent1, kept1 = local_call(
        part(first_body, cx, cy, kz),
        "first_weights",
        [shape((taps, half, chan), BF), shape((taps, half, chan), F32)],
        [pltpu.VMEM(w_first.shape, F32)],
        scalars=1,
    )(side, xp, xs, g1)
    got1 = swap(sent1, core)
    sent1, kept1 = halves(kept1 + got1.astype(F32), two)
    got1 = swap(sent1, two)
    sent2, kept2 = halves(kept2 + got2.astype(F32), two)
    got2 = swap(sent2, two)
    sent1, kept1 = halves(kept1 + got1.astype(F32), one)
    got1 = swap(sent1, one)
    own2, own1 = summed_inner(kept2 + got2.astype(F32), kept1 + got1.astype(F32), levels[3:])
    other2, other1 = swap(own2, two), swap(own1, one)
    own2, own1 = joined(own2, other2, two), joined(own1, other1, one)
    other2, other1 = swap(own2, one), swap(own1, two)
    own2, own1 = joined(own2, other2, one), joined(own1, other1, two)
    step_second, step_first = local_call(
        norm_body,
        "normalize",
        [shape(w_second.shape, F32), shape(w_first.shape, F32)],
        scalars=1,
        out_hbm=(0, 1),
    )(side, own2, swap(own2, core), own1, swap(own1, core))
    return (features, step_first, step_second)


def solution(mesh):
    in_specs = (
        P("gx", "gy", None, None),
        P("gx", "gy", None),
        P(),
        P(),
        P(),
        P(),
        P("gx", "gy", None, None),
    )
    out_specs = (P("gx", "gy", None, None), P(), P())
    return jax.shard_map(
        on_device, mesh=mesh, in_specs=in_specs, out_specs=out_specs, check_vma=False
    )
```

```python
import functools

import jax
import jax.numpy as jnp
from jax import lax
from jax.experimental import pallas as pl
from jax.experimental.pallas import tpu as pltpu
from jax.sharding import PartitionSpec as P

BF = jnp.bfloat16
F32 = jnp.float32
LANES = 128
FIELD_HALO = 3
MASK_HALO = 2


def bit_levels(axes):
    levels = []
    for axis in axes:
        bit = 1
        while bit < lax.axis_size(axis):
            levels.append((axis, bit))
            bit *= 2
    return levels


def swap(part, level):
    axis, bit = level
    return lax.ppermute(part, axis, [(i, i ^ bit) for i in range(lax.axis_size(axis))])


def side_of(level):
    axis, bit = level
    return lax.rem(lax.axis_index(axis) // bit, 2)


def halves(part, level):
    half = part.shape[1] // 2
    side = side_of(level)
    sent = lax.dynamic_slice_in_dim(part, (1 - side) * half, half, 1).astype(BF)
    kept = lax.dynamic_slice_in_dim(part, side * half, half, 1)
    return sent, kept


def joined(own, other, level):
    return jnp.where(
        side_of(level) == 0,
        jnp.concatenate([own, other], axis=1),
        jnp.concatenate([other, own], axis=1),
    )


def summed_inner(second, first, levels):
    middle, final = levels[:-1], levels[-1]
    for level in middle:
        sent2, kept2 = halves(second, level)
        sent1, kept1 = halves(first, level)
        cut = sent2.shape[1]
        got = swap(jnp.concatenate([sent2, sent1], axis=1), level).astype(F32)
        second, first = kept2 + got[:, :cut], kept1 + got[:, cut:]
    cut = second.shape[1]
    both = jnp.concatenate([second, first], axis=1).astype(BF)
    both = (both.astype(F32) + swap(both, final).astype(F32)).astype(BF)
    for level in reversed(middle):
        got = swap(both, level)
        both = jnp.concatenate(
            [joined(both[:, :cut], got[:, :cut], level), joined(both[:, cut:], got[:, cut:], level)],
            axis=1,
        )
        cut *= 2
    return both[:, :cut], both[:, cut:]


def exchange(forward, backward, axis):
    count = lax.axis_size(axis)
    ups = [(i, i + 1) for i in range(count - 1)]
    downs = [(target, source) for source, target in ups]
    return lax.ppermute(forward, axis, ups), lax.ppermute(backward, axis, downs)


def pack_y_body(cx, cy, kz, hfield, hup, hmask, last, first, tile, field, up, mask, square, deep, sems):
    copies = [
        pltpu.make_async_copy(source, target, sems.at[i])
        for i, (source, target) in enumerate(((hmask, mask), (hfield, field), (hup, up)))
    ]
    for copy in copies:
        copy.start()
    cells = cx * cy
    square[...] = jnp.zeros_like(square)
    copies[0].wait()
    square[0:cells, 0 : 2 * kz] = mask[...].reshape(cells, 2 * kz).astype(F32)
    deep[...] = square[...].T
    even = deep[pl.ds(0, kz, stride=2), :]
    odd = deep[pl.ds(1, kz, stride=2), :]
    tile[...] = (even + pltpu.roll(odd, LANES // 2, 1)).astype(BF)
    copies[1].wait()
    copies[2].wait()
    for ref, at_field, at_up in ((last, cy - FIELD_HALO, cy - 1), (first, 0, 0)):
        row = 0
        for rows in (
            field[:, at_field : at_field + FIELD_HALO].reshape(-1, LANES),
            up[:, at_up : at_up + 1].reshape(-1, LANES),
            tile[...],
        ):
            ref[row : row + rows.shape[0]] = rows
            row += rows.shape[0]


def pack_x_body(cx, cy, kz, field, up, tile, left, right, last, first):
    fh = FIELD_HALO
    nf, nu = cx * fh * kz, cx * 2 * kz
    ends_f = [m[0:nf].reshape(cx, fh, kz, LANES) for m in (left, right)]
    ends_u = [m[nf : nf + nu].reshape(cx, 1, 2 * kz, LANES) for m in (left, right)]
    for ref, at_field, at_up in ((last, cx - fh, cx - 1), (first, 0, 0)):
        row = 0
        parts = []
        for r in range(at_field, at_field + fh):
            parts += [ends_f[0][r], field[r], ends_f[1][r]]
        parts += [ends_u[0][at_up], up[at_up], ends_u[1][at_up]]
        parts += [left[nf + nu :], tile[...], right[nf + nu :]]
        for part in parts:
            rows = part.reshape(-1, LANES)
            ref[row : row + rows.shape[0]] = rows
            row += rows.shape[0]


def side_pair(pair, kz, width):
    rows = pair.shape[0]
    depth = lax.rem(lax.broadcasted_iota(jnp.int32, (rows, width), 0), kz)
    above = pltpu.roll(pair[:, :width], rows - 1, 0)
    below = pltpu.roll(pair[:, width:], 1, 0)
    above = jnp.where(depth == kz - 1, 0.0, above)
    below = jnp.where(depth == 0, 0.0, below)
    return above, below


def taps_of(pair, side, at, rows, cols):
    parts = []
    for a in range(3):
        for b in range(3):
            for ref in (pair, side):
                part = ref[pl.ds(at + a, rows), b : b + cols]
                parts.append(part.reshape(-1, part.shape[-1]))
    return jnp.concatenate(parts, axis=1)


def compute_body(
    cx, cy, kz,
    side, field, up, tile, left, right, low, high, w1, b1, w2, b2, w3,
    features, sent, kept,
    xp, xs, hp, hs, act, upf, outf, g2p, g2s, gate, g1, d2, d1,
):
    fh, mh = FIELD_HALO, MASK_HALO
    ex, ey, uy = cx + 2 * fh, cy + 2 * fh, cy + 2
    nf, nu = cx * fh * kz, cx * 2 * kz
    ne, nw = fh * ey * kz, uy * 2 * kz
    xp[fh : fh + cx, fh : fh + cy] = field[...]
    xp[fh : fh + cx, 0:fh] = left[0:nf].reshape(cx, fh, kz, LANES)
    xp[fh : fh + cx, fh + cy :] = right[0:nf].reshape(cx, fh, kz, LANES)
    xp[0:fh] = low[0:ne].reshape(fh, ey, kz, LANES)
    xp[fh + cx :] = high[0:ne].reshape(fh, ey, kz, LANES)

    def fill_side(i, carry):
        rows = xp[i].reshape(ey * kz, LANES).astype(F32)
        depth = lax.rem(lax.broadcasted_iota(jnp.int32, rows.shape, 0), kz)
        lane = lax.broadcasted_iota(jnp.int32, rows.shape, 1)
        above = jnp.where(depth == kz - 1, 0.0, pltpu.roll(rows, ey * kz - 1, 0))
        below = jnp.where(depth == 0, 0.0, pltpu.roll(rows, 1, 0))
        both = jnp.where(lane < LANES // 2, above, below).astype(BF)
        xs[i] = both.reshape(ey, kz, LANES)
        return carry

    lax.fori_loop(0, ex, fill_side, 0)
    span = uy * 2 * kz

    def put_up(x, y, cols, value):
        base = x * span + y * 2 * kz
        upf[base : base + cols * 2 * kz] = value.reshape(-1, LANES).astype(F32)

    put_up(0, 0, uy, low[ne : ne + nw])
    put_up(cx + 1, 0, uy, high[ne : ne + nw])
    for x in range(cx):
        at = nf + x * 2 * kz
        put_up(x + 1, 0, 1, left[at : at + 2 * kz])
        put_up(x + 1, 1, cy, up[x])
        put_up(x + 1, cy + 1, 1, right[at : at + 2 * kz])

    def put_mask(source, sx, sy, x, y):
        for parity in range(2):
            lane = sx * cy + sy + parity * (LANES // 2)
            value = jnp.broadcast_to(source[:, lane : lane + 1], (kz, LANES))
            act[x, y, :, parity * LANES : (parity + 1) * LANES] = value.astype(BF)

    def three(ref, start):
        return [ref[start + i * kz : start + (i + 1) * kz].astype(F32) for i in range(3)]

    rows_mid = [left[nf + nu :].astype(F32), tile[...].astype(F32), right[nf + nu :].astype(F32)]
    rows_low, rows_high = three(low, ne + nw), three(high, ne + nw)
    for x in range(cx + 2 * mh):
        if x < mh:
            sources, sx = rows_low, cx - mh + x
        elif x < mh + cx:
            sources, sx = rows_mid, x - mh
        else:
            sources, sx = rows_high, x - mh - cx
        for y in range(cy):
            put_mask(sources[1], sx, y, x, mh + y)
        for j in range(mh):
            put_mask(sources[0], sx, cy - mh + j, x, j)
            put_mask(sources[2], sx, j, x, mh + cy + j)

    hx, hy = cx + 4, cy + 4
    step = 2

    def first(i, carry):
        at = i * step
        window = taps_of(xp, xs, at, step, hy)
        z = jnp.dot(window, w1[...], preferred_element_type=F32) + b1[...]
        s = jax.nn.sigmoid(z)
        m = act[pl.ds(at, step)].reshape(step * hy * kz, 2 * LANES).astype(F32)
        h = z * s * m
        above, below = side_pair(h, kz, LANES)
        hp[pl.ds(at, step)] = h.astype(BF).reshape(step, hy, kz, 2 * LANES)
        both = jnp.concatenate([above, below], axis=1).astype(BF)
        hs[pl.ds(at, step)] = both.reshape(step, hy, kz, 2 * LANES)

        @pl.when(jnp.logical_and(i >= 2 // step, i < (2 + cx) // step))
        def _():
            factor = m * s * (1.0 + z * (1.0 - s))
            factor = factor.reshape(step, hy, kz, 2 * LANES)[:, 2 : 2 + cy]
            gate[pl.ds(at - 2, step)] = factor

        return carry

    lax.fori_loop(0, hx // step, first, 0)

    def second(i, carry):
        at = i * step
        window = taps_of(hp, hs, at, step, uy)
        z = jnp.dot(window, w2[...], preferred_element_type=F32) + b2[...]
        s = jax.nn.sigmoid(z)
        m = act[pl.ds(at + 1, step), 1 : 1 + uy].reshape(-1, 2 * LANES).astype(F32)
        rows = step * uy * kz
        base = pl.multiple_of(at * span, 8)
        u = jnp.concatenate(
            [upf[pl.ds(base, rows, stride=2), :], upf[pl.ds(base + 1, rows, stride=2), :]], axis=1
        )
        g = u * m * s * (1.0 + z * (1.0 - s))
        gb = g.astype(BF)
        above, below = side_pair(g, kz, LANES)
        g2p[pl.ds(at, step)] = gb.reshape(step, uy, kz, 2 * LANES)
        both = jnp.concatenate([above, below], axis=1).astype(BF)
        g2s[pl.ds(at, step)] = both.reshape(step, uy, kz, 2 * LANES)
        out = z * s * m
        outf[pl.ds(base, rows, stride=2), :] = out[:, :LANES]
        outf[pl.ds(base + 1, rows, stride=2), :] = out[:, LANES:]
        return carry

    lax.fori_loop(0, (cx + 2) // step, second, 0)
    for x in range(cx):
        base = (x + 1) * span + 2 * kz
        rows = outf[base : base + cy * 2 * kz].astype(BF)
        features[x] = rows.reshape(cy, 2 * kz, LANES)

    own = hp[2 : 2 + cx, 2 : 2 + cy].reshape(-1, 2 * LANES)
    turned = own.T
    for a in range(3):
        for b in range(3):
            parts = [
                ref[2 - a : 2 - a + cx, 2 - b : 2 - b + cy].reshape(-1, 2 * LANES)
                for ref in (g2p, g2s)
            ]
            for half, part in enumerate(parts):
                block = jnp.dot(turned, part, preferred_element_type=F32)
                q = [[block[r * LANES : (r + 1) * LANES, c * LANES : (c + 1) * LANES] for c in (0, 1)] for r in (0, 1)]
                t = 9 * a + 3 * b
                if half == 0:
                    d2[t + 1] = q[0][0] + q[1][1]
                    d2[t] = q[0][1]
                    d2[t + 2] = q[1][0]
                else:
                    d2[t] = d2[t] + q[1][0]
                    d2[t + 2] = d2[t + 2] + q[0][1]

    rows = step * cy * kz

    def grad(i, carry):
        at = i * step
        window = taps_of(g2p, g2s, at, step, cy)
        e = jnp.dot(window, w3[...], preferred_element_type=F32)
        g = e * gate[pl.ds(at, step)].reshape(rows, 2 * LANES)
        g1[pl.ds(pl.multiple_of(i * rows, rows), rows)] = g.astype(BF)
        return carry

    lax.fori_loop(0, cx // step, grad, 0)
    right_side = g1[...]
    cells = cx * cy * kz
    half = LANES // 2
    for b in range(3):
        cols = slice(fh - 1 + b, fh - 1 + b + cy)
        parts = [ref[fh - 1 : fh + 1 + cx, cols].reshape(-1, LANES) for ref in (xp, xs)]
        turned = jnp.concatenate(parts, axis=1).T
        for a in range(3):
            at = a * cy * kz
            block = jnp.dot(turned[:, at : at + cells], right_side, preferred_element_type=F32)
            q = [
                [block[r * half : (r + 1) * half, c * LANES : (c + 1) * LANES] for c in (0, 1)]
                for r in range(4)
            ]
            t = 9 * a + 3 * b
            d1[t] = q[0][1] + q[3][0]
            d1[t + 1] = q[0][0] + q[1][1]
            d1[t + 2] = q[1][0] + q[2][1]
    at = 0
    for total in (d2, d1):
        half = total.shape[1] // 2
        mine = pl.multiple_of(side[0] * half, half)
        other = pl.multiple_of((1 - side[0]) * half, half)
        sent[:, at : at + half] = total[:, pl.ds(other, half)].astype(BF)
        kept[:, at : at + half] = total[:, pl.ds(mine, half)]
        at += half


def norm_body(side, own2, other2, own1, other1, out2, out1):
    for own, other, out in ((own2, other2, out2), (own1, other1, out1)):
        half = own.shape[1]
        mine, rest = own[...].astype(F32), other[...].astype(F32)
        total = jnp.sum(mine * mine) + jnp.sum(rest * rest)
        scale = lax.rsqrt(jnp.full((1, LANES), total) / float(out.size) + 1e-06)
        out[:, pl.ds(pl.multiple_of(side[0] * half, half), half)] = mine * scale
        out[:, pl.ds(pl.multiple_of((1 - side[0]) * half, half), half)] = rest * scale


PAIR_TAPS = ((1, 0), (2, 1), (None, 2), (0, None))


def weights_body(first, second, w1, w2, w3):
    taps = second.shape[0]

    def group(g, carry):
        for source, out, turn in ((first, w1, False), (second, w2, False), (second, w3, True)):
            depth, width = source.shape[1:]
            if turn:
                block = [source[taps - 1 - 3 * g - c].astype(F32).T.astype(BF) for c in range(3)]
            else:
                block = [source[3 * g + c] for c in range(3)]
            none = jnp.zeros((depth, width), BF)
            for r, row in enumerate(PAIR_TAPS):
                at = pl.multiple_of(g * 4 * depth + r * depth, depth)
                for c, tap in enumerate(row):
                    value = none if tap is None else block[tap]
                    out[pl.ds(at, depth), c * width : (c + 1) * width] = value
        return carry

    lax.fori_loop(0, taps // 3, group, 0)


def local_call(body, name, out, scratch=(), scalars=0, in_hbm=(), out_hbm=(), limit=24):
    def call(*args):
        vmem = pl.BlockSpec(memory_space=pltpu.VMEM)
        plain = pl.BlockSpec()
        hbm = pl.BlockSpec(memory_space=pltpu.HBM)
        ins = [
            pl.BlockSpec(memory_space=pltpu.SMEM) if i < scalars else hbm if i in in_hbm else vmem
            for i in range(len(args))
        ]
        held = [
            a
            if i < scalars
            else pltpu.with_memory_space_constraint(a, pltpu.HBM if i in in_hbm else pltpu.VMEM)
            for i, a in enumerate(args)
        ]
        outs = [o if i in out_hbm else pltpu.VMEM(o.shape, o.dtype) for i, o in enumerate(out)]
        return pl.pallas_call(
            body,
            out_shape=outs,
            in_specs=ins,
            out_specs=[plain if i in out_hbm else vmem for i in range(len(out))],
            scratch_shapes=list(scratch),
            compiler_params=pltpu.CompilerParams(vmem_limit_bytes=limit << 20),
            name=name,
        )(*held)

    return call


def on_device(volume, basin_mask, w_first, b_first, w_second, b_second, upstream):
    cx, cy, kz, _ = volume.shape
    taps, _, chan = w_first.shape
    part = functools.partial
    shape = jax.ShapeDtypeStruct
    levels = bit_levels(("gx", "gy"))
    core, one, two = levels[:3]
    side = side_of(core).astype(jnp.int32).reshape(1)
    ex, ey, uy = cx + 2 * FIELD_HALO, cy + 2 * FIELD_HALO, cy + 2
    rows_y = cx * FIELD_HALO * kz + cx * 2 * kz + kz
    last, first, tile, field, up = local_call(
        part(pack_y_body, cx, cy, kz),
        "pack_y",
        [shape((rows_y, LANES), BF)] * 2
        + [shape((kz, LANES), BF), shape(volume.shape, BF), shape(upstream.shape, BF)],
        [pltpu.VMEM(basin_mask.shape, jnp.int32)]
        + [pltpu.VMEM((LANES, LANES), F32)] * 2
        + [pltpu.SemaphoreType.DMA((3,))],
        in_hbm=(0, 1, 2),
    )(volume, upstream, basin_mask)
    left, right = exchange(last, first, "gy")
    w1, w2, w3 = local_call(
        weights_body,
        "weights",
        [
            shape((4 * taps // 3 * w_first.shape[1], 2 * chan), BF),
            shape((4 * taps // 3 * chan, 2 * chan), BF),
            shape((4 * taps // 3 * chan, 2 * chan), BF),
        ],
    )(w_first, w_second)
    rows_x = FIELD_HALO * ey * kz + uy * 2 * kz + 3 * kz
    last, first = local_call(
        part(pack_x_body, cx, cy, kz), "pack_x", [shape((rows_x, LANES), BF)] * 2
    )(field, up, tile, left, right)
    low, high = exchange(last, first, "gx")
    b1 = jnp.concatenate([b_first, b_first]).reshape(1, -1)
    b2 = jnp.concatenate([b_second, b_second]).reshape(1, -1)
    cut = chan // 2
    rows = cut + w_first.shape[1] // 2
    pairs = (kz, 2 * chan)
    features, sent, kept = local_call(
        part(compute_body, cx, cy, kz),
        "compute",
        [
            shape((cx, cy, 2 * kz, chan), BF),
            shape((taps, rows, chan), BF),
            shape((taps, rows, chan), F32),
        ],
        [
            pltpu.VMEM((ex, ey, kz, LANES), BF),
            pltpu.VMEM((ex, ey, kz, LANES), BF),
            pltpu.VMEM((cx + 4, cy + 4, *pairs), BF),
            pltpu.VMEM((cx + 4, cy + 4, *pairs), BF),
            pltpu.VMEM((cx + 4, cy + 4, *pairs), BF),
            pltpu.VMEM(((cx + 2) * uy * 2 * kz, LANES), F32),
            pltpu.VMEM(((cx + 2) * uy * 2 * kz, LANES), F32),
            pltpu.VMEM((cx + 2, uy, *pairs), BF),
            pltpu.VMEM((cx + 2, uy, *pairs), BF),
            pltpu.VMEM((cx, cy, *pairs), F32),
            pltpu.VMEM((cx * cy * kz, 2 * chan), BF),
            pltpu.VMEM(w_second.shape, F32),
            pltpu.VMEM(w_first.shape, F32),
        ],
        scalars=1,
        limit=32,
    )(side, field, up, tile, left, right, low, high, w1, b1, w2, b2, w3)
    total = kept + swap(sent, core).astype(F32)
    sent2, kept2 = halves(total[:, :cut], one)
    sent1, kept1 = halves(total[:, cut:], two)
    got2, got1 = lax.optimization_barrier((swap(sent2, one), swap(sent1, two)))
    sent2, kept2 = halves(kept2 + got2.astype(F32), two)
    sent1, kept1 = halves(kept1 + got1.astype(F32), one)
    got2, got1 = lax.optimization_barrier((swap(sent2, two), swap(sent1, one)))
    own2, own1 = summed_inner(kept2 + got2.astype(F32), kept1 + got1.astype(F32), levels[3:])
    other2, other1 = lax.optimization_barrier((swap(own2, two), swap(own1, one)))
    own2, own1 = joined(own2, other2, two), joined(own1, other1, one)
    other2, other1 = lax.optimization_barrier((swap(own2, one), swap(own1, two)))
    own2, own1 = joined(own2, other2, one), joined(own1, other1, two)
    step_second, step_first = local_call(
        norm_body,
        "normalize",
        [shape(w_second.shape, F32), shape(w_first.shape, F32)],
        scalars=1,
        out_hbm=(0, 1),
    )(side, own2, swap(own2, core), own1, swap(own1, core))
    return (features, step_first, step_second)


def solution(mesh):
    in_specs = (
        P("gx", "gy", None, None),
        P("gx", "gy", None),
        P(),
        P(),
        P(),
        P(),
        P("gx", "gy", None, None),
    )
    out_specs = (P("gx", "gy", None, None), P(), P())
    return jax.shard_map(
        on_device, mesh=mesh, in_specs=in_specs, out_specs=out_specs, check_vma=False
    )
```

```python
import functools

import jax
import jax.numpy as jnp
from jax import lax
from jax.experimental import pallas as pl
from jax.experimental.pallas import tpu as pltpu
from jax.sharding import PartitionSpec as P

BF = jnp.bfloat16
F32 = jnp.float32
LANES = 128
FIELD_HALO = 3
MASK_HALO = 2


def bit_levels(axes):
    levels = []
    for axis in axes:
        bit = 1
        while bit < lax.axis_size(axis):
            levels.append((axis, bit))
            bit *= 2
    return levels


def swap(part, level):
    axis, bit = level
    return lax.ppermute(part, axis, [(i, i ^ bit) for i in range(lax.axis_size(axis))])


def side_of(level):
    axis, bit = level
    return lax.rem(lax.axis_index(axis) // bit, 2)


def halves(part, level):
    half = part.shape[0] // 2
    side = side_of(level)
    sent = lax.dynamic_slice_in_dim(part, (1 - side) * half, half, 0).astype(BF)
    kept = lax.dynamic_slice_in_dim(part, side * half, half, 0)
    return sent, kept


def joined(own, other, level):
    return jnp.where(
        side_of(level) == 0,
        jnp.concatenate([own, other], axis=0),
        jnp.concatenate([other, own], axis=0),
    )


def summed_everywhere(total, levels):
    one, two, middle, final = levels[0], levels[1], levels[2:-1], levels[-1]
    cut = total.shape[0] // 2
    parts = [total[:cut], total[cut:]]
    for order in ((one, two), (two, one)):
        split = [halves(part, level) for part, level in zip(parts, order)]
        got = lax.optimization_barrier(
            [swap(sent, level) for (sent, _), level in zip(split, order)]
        )
        parts = [kept + other.astype(F32) for (_, kept), other in zip(split, got)]
    both = jnp.concatenate(parts, axis=0)
    for level in middle:
        sent, kept = halves(both, level)
        both = kept + swap(sent, level).astype(F32)
    both = both.astype(BF)
    both = (both.astype(F32) + swap(both, final).astype(F32)).astype(BF)
    for level in reversed(middle):
        both = joined(both, swap(both, level), level)
    cut = both.shape[0] // 2
    parts = [both[:cut], both[cut:]]
    for order in ((two, one), (one, two)):
        got = lax.optimization_barrier([swap(part, level) for part, level in zip(parts, order)])
        parts = [joined(own, other, level) for own, other, level in zip(parts, got, order)]
    return parts


def exchange(inner, outer, axis):
    count = lax.axis_size(axis)
    pairs = [(i, i + 1) for i in range(1, count - 1, 2)]
    outer = lax.ppermute(outer, axis, pairs + [(b, a) for a, b in pairs])
    inner = lax.ppermute(inner, axis, [(i, i ^ 1) for i in range(count)])
    return inner, outer


def ends_of(odd, inner, outer):
    first, second = inner[...], outer[...]
    return jnp.where(odd, first, second), jnp.where(odd, second, first)


def pack_y_body(
    cx, cy, kz, odd, hfield, hup, hmask, inner, outer, tile, field, up, mask, square, deep, sems
):
    copies = [
        pltpu.make_async_copy(source, target, sems.at[i])
        for i, (source, target) in enumerate(((hmask, mask), (hfield, field), (hup, up)))
    ]
    for copy in copies:
        copy.start()
    cells = cx * cy
    square[...] = jnp.zeros_like(square)
    copies[0].wait()
    square[0:cells, 0 : 2 * kz] = mask[...].reshape(cells, 2 * kz).astype(F32)
    deep[...] = square[...].T
    at_even = deep[pl.ds(0, kz, stride=2), :]
    at_odd = deep[pl.ds(1, kz, stride=2), :]
    tile[...] = (at_even + pltpu.roll(at_odd, LANES // 2, 1)).astype(BF)
    copies[1].wait()
    copies[2].wait()
    for ref, end in ((inner, 1 - odd[0]), (outer, odd[0])):
        row = 0
        for rows in (
            field[:, pl.ds(end * (cy - FIELD_HALO), FIELD_HALO)].reshape(-1, LANES),
            up[:, pl.ds(end * (cy - 1), 1)].reshape(-1, LANES),
            tile[...],
        ):
            ref[row : row + rows.shape[0]] = rows
            row += rows.shape[0]


def pack_x_body(
    cx, cy, kz, odd, odd_y, field, up, tile, inner_y, outer_y, inner, outer, left, right
):
    left[...], right[...] = ends_of(odd_y[0] == 1, inner_y, outer_y)
    fh = FIELD_HALO
    nf, nu = cx * fh * kz, cx * 2 * kz
    for ref, end in ((inner, 1 - odd[0]), (outer, odd[0])):
        at_field, at_up = end * (cx - fh), end * (cx - 1)
        row = 0
        parts = []
        for r in range(fh):
            at = pl.multiple_of((at_field + r) * fh * kz, kz)
            parts += [left[pl.ds(at, fh * kz)], field[at_field + r], right[pl.ds(at, fh * kz)]]
        at = pl.multiple_of(nf + at_up * 2 * kz, kz)
        parts += [left[pl.ds(at, 2 * kz)], up[at_up], right[pl.ds(at, 2 * kz)]]
        parts += [left[nf + nu :], tile[...], right[nf + nu :]]
        for part in parts:
            rows = part.reshape(-1, LANES)
            ref[row : row + rows.shape[0]] = rows
            row += rows.shape[0]


def side_pair(pair, kz, width):
    rows = pair.shape[0]
    depth = lax.rem(lax.broadcasted_iota(jnp.int32, (rows, width), 0), kz)
    above = pltpu.roll(pair[:, :width], rows - 1, 0)
    below = pltpu.roll(pair[:, width:], 1, 0)
    above = jnp.where(depth == kz - 1, 0.0, above)
    below = jnp.where(depth == 0, 0.0, below)
    return above, below


def taps_of(pair, side, at, rows, cols):
    parts = []
    for a in range(3):
        for b in range(3):
            for ref in (pair, side):
                part = ref[pl.ds(at + a, rows), b : b + cols]
                parts.append(part.reshape(-1, part.shape[-1]))
    return jnp.concatenate(parts, axis=1)


def compute_body(
    cx, cy, kz,
    side, field, up, tile, left, right, inner, outer, w1, b1, w2, b2, w3,
    features, sent, kept,
    low, high, xp, xs, hp, hs, act, upf, outf, g2p, g2s, gate, g1, d2, d1,
):
    low[...], high[...] = ends_of(side[0] == 1, inner, outer)
    fh, mh = FIELD_HALO, MASK_HALO
    ex, ey, uy = cx + 2 * fh, cy + 2 * fh, cy + 2
    nf, nu = cx * fh * kz, cx * 2 * kz
    ne, nw = fh * ey * kz, uy * 2 * kz
    xp[fh : fh + cx, fh : fh + cy] = field[...]
    xp[fh : fh + cx, 0:fh] = left[0:nf].reshape(cx, fh, kz, LANES)
    xp[fh : fh + cx, fh + cy :] = right[0:nf].reshape(cx, fh, kz, LANES)
    xp[0:fh] = low[0:ne].reshape(fh, ey, kz, LANES)
    xp[fh + cx :] = high[0:ne].reshape(fh, ey, kz, LANES)

    def fill_side(i, carry):
        rows = xp[i].reshape(ey * kz, LANES).astype(F32)
        depth = lax.rem(lax.broadcasted_iota(jnp.int32, rows.shape, 0), kz)
        lane = lax.broadcasted_iota(jnp.int32, rows.shape, 1)
        above = jnp.where(depth == kz - 1, 0.0, pltpu.roll(rows, ey * kz - 1, 0))
        below = jnp.where(depth == 0, 0.0, pltpu.roll(rows, 1, 0))
        both = jnp.where(lane < LANES // 2, above, below).astype(BF)
        xs[i] = both.reshape(ey, kz, LANES)
        return carry

    lax.fori_loop(0, ex, fill_side, 0)
    span = uy * 2 * kz

    def put_up(x, y, cols, value):
        base = x * span + y * 2 * kz
        upf[base : base + cols * 2 * kz] = value.reshape(-1, LANES).astype(F32)

    put_up(0, 0, uy, low[ne : ne + nw])
    put_up(cx + 1, 0, uy, high[ne : ne + nw])
    for x in range(cx):
        at = nf + x * 2 * kz
        put_up(x + 1, 0, 1, left[at : at + 2 * kz])
        put_up(x + 1, 1, cy, up[x])
        put_up(x + 1, cy + 1, 1, right[at : at + 2 * kz])

    def put_mask(source, sx, sy, x, y):
        for parity in range(2):
            lane = sx * cy + sy + parity * (LANES // 2)
            value = jnp.broadcast_to(source[:, lane : lane + 1], (kz, LANES))
            act[x, y, :, parity * LANES : (parity + 1) * LANES] = value.astype(BF)

    def three(ref, start):
        return [ref[start + i * kz : start + (i + 1) * kz].astype(F32) for i in range(3)]

    rows_mid = [left[nf + nu :].astype(F32), tile[...].astype(F32), right[nf + nu :].astype(F32)]
    rows_low, rows_high = three(low, ne + nw), three(high, ne + nw)
    for x in range(cx + 2 * mh):
        if x < mh:
            sources, sx = rows_low, cx - mh + x
        elif x < mh + cx:
            sources, sx = rows_mid, x - mh
        else:
            sources, sx = rows_high, x - mh - cx
        for y in range(cy):
            put_mask(sources[1], sx, y, x, mh + y)
        for j in range(mh):
            put_mask(sources[0], sx, cy - mh + j, x, j)
            put_mask(sources[2], sx, j, x, mh + cy + j)

    hx, hy = cx + 4, cy + 4
    step = 2

    def first(i, carry):
        at = i * step
        window = taps_of(xp, xs, at, step, hy)
        z = jnp.dot(window, w1[...], preferred_element_type=F32) + b1[...]
        s = jax.nn.sigmoid(z)
        m = act[pl.ds(at, step)].reshape(step * hy * kz, 2 * LANES).astype(F32)
        h = z * s * m
        above, below = side_pair(h, kz, LANES)
        hp[pl.ds(at, step)] = h.astype(BF).reshape(step, hy, kz, 2 * LANES)
        both = jnp.concatenate([above, below], axis=1).astype(BF)
        hs[pl.ds(at, step)] = both.reshape(step, hy, kz, 2 * LANES)

        @pl.when(jnp.logical_and(i >= 2 // step, i < (2 + cx) // step))
        def _():
            factor = m * s * (1.0 + z * (1.0 - s))
            factor = factor.reshape(step, hy, kz, 2 * LANES)[:, 2 : 2 + cy]
            gate[pl.ds(at - 2, step)] = factor

        return carry

    lax.fori_loop(0, hx // step, first, 0)

    def second(i, carry):
        at = i * step
        window = taps_of(hp, hs, at, step, uy)
        z = jnp.dot(window, w2[...], preferred_element_type=F32) + b2[...]
        s = jax.nn.sigmoid(z)
        m = act[pl.ds(at + 1, step), 1 : 1 + uy].reshape(-1, 2 * LANES).astype(F32)
        rows = step * uy * kz
        base = pl.multiple_of(at * span, 8)
        u = jnp.concatenate(
            [upf[pl.ds(base, rows, stride=2), :], upf[pl.ds(base + 1, rows, stride=2), :]], axis=1
        )
        g = u * m * s * (1.0 + z * (1.0 - s))
        gb = g.astype(BF)
        above, below = side_pair(g, kz, LANES)
        g2p[pl.ds(at, step)] = gb.reshape(step, uy, kz, 2 * LANES)
        both = jnp.concatenate([above, below], axis=1).astype(BF)
        g2s[pl.ds(at, step)] = both.reshape(step, uy, kz, 2 * LANES)
        out = z * s * m
        outf[pl.ds(base, rows, stride=2), :] = out[:, :LANES]
        outf[pl.ds(base + 1, rows, stride=2), :] = out[:, LANES:]
        return carry

    lax.fori_loop(0, (cx + 2) // step, second, 0)
    for x in range(cx):
        base = (x + 1) * span + 2 * kz
        rows = outf[base : base + cy * 2 * kz].astype(BF)
        features[x] = rows.reshape(cy, 2 * kz, LANES)

    own = hp[2 : 2 + cx, 2 : 2 + cy].reshape(-1, 2 * LANES)
    turned = own.T
    for a in range(3):
        for b in range(3):
            parts = [
                ref[2 - a : 2 - a + cx, 2 - b : 2 - b + cy].reshape(-1, 2 * LANES)
                for ref in (g2p, g2s)
            ]
            for half, part in enumerate(parts):
                block = jnp.dot(turned, part, preferred_element_type=F32)
                q = [[block[r * LANES : (r + 1) * LANES, c * LANES : (c + 1) * LANES] for c in (0, 1)] for r in (0, 1)]
                t = 9 * a + 3 * b
                if half == 0:
                    d2[t + 1] = q[0][0] + q[1][1]
                    d2[t] = q[0][1]
                    d2[t + 2] = q[1][0]
                else:
                    d2[t] = d2[t] + q[1][0]
                    d2[t + 2] = d2[t + 2] + q[0][1]

    rows = step * cy * kz

    def grad(i, carry):
        at = i * step
        window = taps_of(g2p, g2s, at, step, cy)
        e = jnp.dot(window, w3[...], preferred_element_type=F32)
        g = e * gate[pl.ds(at, step)].reshape(rows, 2 * LANES)
        g1[pl.ds(pl.multiple_of(i * rows, rows), rows)] = g.astype(BF)
        return carry

    lax.fori_loop(0, cx // step, grad, 0)
    right_side = g1[...]
    cells = cx * cy * kz
    half = LANES // 2
    for b in range(3):
        cols = slice(fh - 1 + b, fh - 1 + b + cy)
        parts = [ref[fh - 1 : fh + 1 + cx, cols].reshape(-1, LANES) for ref in (xp, xs)]
        turned = jnp.concatenate(parts, axis=1).T
        for a in range(3):
            at = a * cy * kz
            block = jnp.dot(turned[:, at : at + cells], right_side, preferred_element_type=F32)
            q = [
                [block[r * half : (r + 1) * half, c * LANES : (c + 1) * LANES] for c in (0, 1)]
                for r in range(4)
            ]
            t = 9 * a + 3 * b
            d1[t] = q[0][1] + q[3][0]
            d1[t + 1] = q[0][0] + q[1][1]
            d1[t + 2] = q[1][0] + q[2][1]
    at = 0
    for total in (d2, d1):
        half = total.shape[1] // 2
        mine = pl.multiple_of(side[0] * half, half)
        other = pl.multiple_of((1 - side[0]) * half, half)
        sent[:, at : at + half] = total[:, pl.ds(other, half)].astype(BF)
        kept[:, at : at + half] = total[:, pl.ds(mine, half)]
        at += half


def norm_body(side, own_a, own_b, other_a, other_b, out2, out1, held2, held1, sems):
    taps = out2.shape[0]
    split = own_a.shape[0]
    rows_of = held2.shape[1] // 2, held1.shape[1] // 2
    stride = sum(rows_of)

    def rows(pair, start, count):
        low, high = pair
        parts = []
        if start < split:
            parts.append(low[start : min(start + count, split)])
        if start + count > split:
            parts.append(high[max(start, split) - split : start + count - split])
        return jnp.concatenate(parts, axis=0).astype(F32)

    def spans():
        for t in range(taps):
            for i, at in ((0, t * stride), (1, t * stride + rows_of[0])):
                yield t, i, at

    squares = [jnp.zeros((8, LANES), F32), jnp.zeros((8, LANES), F32)]
    for t, i, at in spans():
        for pair in ((own_a, own_b), (other_a, other_b)):
            value = rows(pair, at, rows_of[i])
            squares[i] += jnp.sum((value * value).reshape(-1, 8, LANES), axis=0)
    scales = [
        lax.rsqrt(jnp.full((1, LANES), jnp.sum(total)) / float(out.size) + 1e-06)
        for total, out in zip(squares, (out2, out1))
    ]
    group = taps // 3
    copies = []
    for t, i, at in spans():
        held, count = (held2, held1)[i], rows_of[i]
        mine = pl.multiple_of(side[0] * count, count)
        rest = pl.multiple_of((1 - side[0]) * count, count)
        held[t, pl.ds(mine, count)] = rows((own_a, own_b), at, count) * scales[i]
        held[t, pl.ds(rest, count)] = rows((other_a, other_b), at, count) * scales[i]
        if i == 1 and (t + 1) % group == 0:
            span = pl.ds(t + 1 - group, group)
            for held, out in ((held2, out2), (held1, out1)):
                copy = pltpu.make_async_copy(held.at[span], out.at[span], sems.at[len(copies)])
                copy.start()
                copies.append(copy)
    for copy in copies:
        copy.wait()


PAIR_TAPS = ((1, 0), (2, 1), (None, 2), (0, None))


def weights_body(first, second, w1, w2, w3):
    taps = second.shape[0]

    def group(g, carry):
        for source, out, turn in ((first, w1, False), (second, w2, False), (second, w3, True)):
            depth, width = source.shape[1:]
            if turn:
                block = [source[taps - 1 - 3 * g - c].astype(F32).T.astype(BF) for c in range(3)]
            else:
                block = [source[3 * g + c] for c in range(3)]
            none = jnp.zeros((depth, width), BF)
            for r, row in enumerate(PAIR_TAPS):
                at = pl.multiple_of(g * 4 * depth + r * depth, depth)
                for c, tap in enumerate(row):
                    value = none if tap is None else block[tap]
                    out[pl.ds(at, depth), c * width : (c + 1) * width] = value
        return carry

    lax.fori_loop(0, taps // 3, group, 0)


def local_call(body, name, out, scratch=(), scalars=0, in_hbm=(), out_hbm=(), limit=24):
    def call(*args):
        vmem = pl.BlockSpec(memory_space=pltpu.VMEM)
        hbm = pl.BlockSpec(memory_space=pltpu.HBM)
        ins = [
            pl.BlockSpec(memory_space=pltpu.SMEM) if i < scalars else hbm if i in in_hbm else vmem
            for i in range(len(args))
        ]
        held = [
            a
            if i < scalars
            else pltpu.with_memory_space_constraint(a, pltpu.HBM if i in in_hbm else pltpu.VMEM)
            for i, a in enumerate(args)
        ]
        outs = [
            (pltpu.HBM if i in out_hbm else pltpu.VMEM)(o.shape, o.dtype) for i, o in enumerate(out)
        ]
        return pl.pallas_call(
            body,
            out_shape=outs,
            in_specs=ins,
            out_specs=[hbm if i in out_hbm else vmem for i in range(len(out))],
            scratch_shapes=list(scratch),
            compiler_params=pltpu.CompilerParams(vmem_limit_bytes=limit << 20),
            name=name,
        )(*held)

    return call


def on_device(volume, basin_mask, w_first, b_first, w_second, b_second, upstream):
    cx, cy, kz, _ = volume.shape
    taps, _, chan = w_first.shape
    part = functools.partial
    shape = jax.ShapeDtypeStruct
    levels = bit_levels(("gx", "gy"))
    core = levels[0]
    side = side_of(core).astype(jnp.int32).reshape(1)
    odd_y = side_of(("gy", 1)).astype(jnp.int32).reshape(1)
    ex, ey, uy = cx + 2 * FIELD_HALO, cy + 2 * FIELD_HALO, cy + 2
    rows_y = cx * FIELD_HALO * kz + cx * 2 * kz + kz
    inner, outer, tile, field, up = local_call(
        part(pack_y_body, cx, cy, kz),
        "pack_y",
        [shape((rows_y, LANES), BF)] * 2
        + [shape((kz, LANES), BF), shape(volume.shape, BF), shape(upstream.shape, BF)],
        [pltpu.VMEM(basin_mask.shape, jnp.int32)]
        + [pltpu.VMEM((LANES, LANES), F32)] * 2
        + [pltpu.SemaphoreType.DMA((3,))],
        scalars=1,
        in_hbm=(1, 2, 3),
    )(odd_y, volume, upstream, basin_mask)
    inner, outer = exchange(inner, outer, "gy")
    w1, w2, w3 = local_call(
        weights_body,
        "weights",
        [
            shape((4 * taps // 3 * w_first.shape[1], 2 * chan), BF),
            shape((4 * taps // 3 * chan, 2 * chan), BF),
            shape((4 * taps // 3 * chan, 2 * chan), BF),
        ],
    )(w_first, w_second)
    rows_x = FIELD_HALO * ey * kz + uy * 2 * kz + 3 * kz
    inner, outer, left, right = local_call(
        part(pack_x_body, cx, cy, kz),
        "pack_x",
        [shape((rows_x, LANES), BF)] * 2 + [shape((rows_y, LANES), BF)] * 2,
        scalars=2,
    )(side, odd_y, field, up, tile, inner, outer)
    inner, outer = exchange(inner, outer, "gx")
    b1 = jnp.concatenate([b_first, b_first]).reshape(1, -1)
    b2 = jnp.concatenate([b_second, b_second]).reshape(1, -1)
    rows = chan // 2 + w_first.shape[1] // 2
    pairs = (kz, 2 * chan)
    features, sent, kept = local_call(
        part(compute_body, cx, cy, kz),
        "compute",
        [
            shape((cx, cy, 2 * kz, chan), BF),
            shape((taps, rows, chan), BF),
            shape((taps, rows, chan), F32),
        ],
        [pltpu.VMEM((rows_x, LANES), BF)] * 2
        + [
            pltpu.VMEM((ex, ey, kz, LANES), BF),
            pltpu.VMEM((ex, ey, kz, LANES), BF),
            pltpu.VMEM((cx + 4, cy + 4, *pairs), BF),
            pltpu.VMEM((cx + 4, cy + 4, *pairs), BF),
            pltpu.VMEM((cx + 4, cy + 4, *pairs), BF),
            pltpu.VMEM(((cx + 2) * uy * 2 * kz, LANES), F32),
            pltpu.VMEM(((cx + 2) * uy * 2 * kz, LANES), F32),
            pltpu.VMEM((cx + 2, uy, *pairs), BF),
            pltpu.VMEM((cx + 2, uy, *pairs), BF),
            pltpu.VMEM((cx, cy, *pairs), F32),
            pltpu.VMEM((cx * cy * kz, 2 * chan), BF),
            pltpu.VMEM(w_second.shape, F32),
            pltpu.VMEM(w_first.shape, F32),
        ],
        scalars=1,
        limit=32,
    )(side, field, up, tile, left, right, inner, outer, w1, b1, w2, b2, w3)
    total = kept.reshape(-1, chan) + swap(sent.reshape(-1, chan), core).astype(F32)
    own = summed_everywhere(total, levels[1:])
    other = [swap(part_of, core) for part_of in own]
    step_second, step_first = local_call(
        norm_body,
        "normalize",
        [shape(w_second.shape, F32), shape(w_first.shape, F32)],
        [
            pltpu.VMEM(w_second.shape, F32),
            pltpu.VMEM(w_first.shape, F32),
            pltpu.SemaphoreType.DMA((6,)),
        ],
        scalars=1,
        out_hbm=(0, 1),
    )(side, *own, *other)
    return (features, step_first, step_second)


def solution(mesh):
    in_specs = (
        P("gx", "gy", None, None),
        P("gx", "gy", None),
        P(),
        P(),
        P(),
        P(),
        P("gx", "gy", None, None),
    )
    out_specs = (P("gx", "gy", None, None), P(), P())
    return jax.shard_map(
        on_device, mesh=mesh, in_specs=in_specs, out_specs=out_specs, check_vma=False
    )
```

```python
import functools

import jax
import jax.numpy as jnp
from jax import lax
from jax.experimental import pallas as pl
from jax.experimental.pallas import tpu as pltpu
from jax.sharding import PartitionSpec as P

BF = jnp.bfloat16
F32 = jnp.float32
LANES = 128
FIELD_HALO = 3
MASK_HALO = 2


def bit_levels(axes):
    levels = []
    for axis in axes:
        bit = 1
        while bit < lax.axis_size(axis):
            levels.append((axis, bit))
            bit *= 2
    return levels


def swap(part, level):
    axis, bit = level
    return lax.ppermute(part, axis, [(i, i ^ bit) for i in range(lax.axis_size(axis))])


def side_of(level):
    axis, bit = level
    return lax.rem(lax.axis_index(axis) // bit, 2)


def halves(part, level):
    half = part.shape[0] // 2
    side = side_of(level)
    sent = lax.dynamic_slice_in_dim(part, (1 - side) * half, half, 0).astype(BF)
    kept = lax.dynamic_slice_in_dim(part, side * half, half, 0)
    return sent, kept


def joined(own, other, level):
    return jnp.where(
        side_of(level) == 0,
        jnp.concatenate([own, other], axis=0),
        jnp.concatenate([other, own], axis=0),
    )


def summed_everywhere(total, levels):
    one, two, middle, final = levels[0], levels[1], levels[2:-1], levels[-1]
    cut = total.shape[0] // 2
    parts = [total[:cut], total[cut:]]
    for order in ((one, two), (two, one)):
        split = [halves(part, level) for part, level in zip(parts, order)]
        got = lax.optimization_barrier(
            [swap(sent, level) for (sent, _), level in zip(split, order)]
        )
        parts = [kept + other.astype(F32) for (_, kept), other in zip(split, got)]
    both = jnp.concatenate(parts, axis=0)
    for level in middle:
        sent, kept = halves(both, level)
        both = kept + swap(sent, level).astype(F32)
    both = both.astype(BF)
    both = (both.astype(F32) + swap(both, final).astype(F32)).astype(BF)
    for level in reversed(middle):
        both = joined(both, swap(both, level), level)
    cut = both.shape[0] // 2
    parts = [both[:cut], both[cut:]]
    for order in ((two, one), (one, two)):
        got = lax.optimization_barrier([swap(part, level) for part, level in zip(parts, order)])
        parts = [joined(own, other, level) for own, other, level in zip(parts, got, order)]
    return parts


def exchange(inner, outer, axis):
    count = lax.axis_size(axis)
    pairs = [(i, i + 1) for i in range(1, count - 1, 2)]
    outer = lax.ppermute(outer, axis, pairs + [(b, a) for a, b in pairs])
    inner = lax.ppermute(inner, axis, [(i, i ^ 1) for i in range(count)])
    return inner, outer


def ends_of(odd, inner, outer):
    first, second = inner[...], outer[...]
    return jnp.where(odd, first, second), jnp.where(odd, second, first)


def put_rows(ref, parts):
    row = 0
    for part in parts:
        rows = part.reshape(-1, LANES)
        ref[row : row + rows.shape[0]] = rows
        row += rows.shape[0]


def pack_own_body(
    cx, cy, kz, odd, odd_y, hfield, hup, hmask, hfirst, hsecond,
    inner_y, outer_y, inner_x, outer_x, tile, field, up, w_first, w_second,
    mask, square, deep, sems,
):
    fh = FIELD_HALO
    pairs = (
        (hmask, mask),
        (hfield, field),
        (hup, up),
        (hfirst, w_first),
        (hsecond, w_second),
    )
    copies = [
        pltpu.make_async_copy(source, target, sems.at[i])
        for i, (source, target) in enumerate(pairs)
    ]
    for copy in copies:
        copy.start()
    cells = cx * cy
    square[...] = jnp.zeros_like(square)
    copies[0].wait()
    square[0:cells, 0 : 2 * kz] = mask[...].reshape(cells, 2 * kz).astype(F32)
    deep[...] = square[...].T
    at_even = deep[pl.ds(0, kz, stride=2), :]
    at_odd = deep[pl.ds(1, kz, stride=2), :]
    tile[...] = (at_even + pltpu.roll(at_odd, LANES // 2, 1)).astype(BF)
    copies[1].wait()
    copies[2].wait()
    for ref, end in ((inner_y, 1 - odd_y[0]), (outer_y, odd_y[0])):
        put_rows(
            ref,
            (field[:, pl.ds(end * (cy - fh), fh)], up[:, pl.ds(end * (cy - 1), 1)], tile[...]),
        )
    for ref, end in ((inner_x, 1 - odd[0]), (outer_x, odd[0])):
        put_rows(
            ref, (field[pl.ds(end * (cx - fh), fh)], up[pl.ds(end * (cx - 1), 1)], tile[...])
        )
    copies[3].wait()
    copies[4].wait()


def pack_corner_body(cx, cy, kz, odd, odd_y, inner_y, outer_y, inner, outer, left, right):
    left[...], right[...] = ends_of(odd_y[0] == 1, inner_y, outer_y)
    fh = FIELD_HALO
    nf, nu = cx * fh * kz, cx * 2 * kz
    for ref, end in ((inner, 1 - odd[0]), (outer, odd[0])):
        parts = []
        for r in range(fh):
            at = pl.multiple_of((end * (cx - fh) + r) * fh * kz, kz)
            parts += [left[pl.ds(at, fh * kz)], right[pl.ds(at, fh * kz)]]
        at = pl.multiple_of(nf + end * (cx - 1) * 2 * kz, kz)
        parts += [left[pl.ds(at, 2 * kz)], right[pl.ds(at, 2 * kz)]]
        parts += [left[nf + nu :], right[nf + nu :]]
        put_rows(ref, parts)


def side_pair(pair, kz, width):
    rows = pair.shape[0]
    depth = lax.rem(lax.broadcasted_iota(jnp.int32, (rows, width), 0), kz)
    above = pltpu.roll(pair[:, :width], rows - 1, 0)
    below = pltpu.roll(pair[:, width:], 1, 0)
    above = jnp.where(depth == kz - 1, 0.0, above)
    below = jnp.where(depth == 0, 0.0, below)
    return above, below


def taps_of(pair, side, at, rows, cols):
    parts = []
    for a in range(3):
        for b in range(3):
            for ref in (pair, side):
                part = ref[pl.ds(at + a, rows), b : b + cols]
                parts.append(part.reshape(-1, part.shape[-1]))
    return jnp.concatenate(parts, axis=1)


def compute_body(
    cx, cy, kz,
    side, field, up, tile, left, right, inner_x, outer_x, inner, outer, w1, b1, w2, b2, w3,
    features, sent, kept,
    low, high, low_ends, high_ends,
    xp, xs, hp, hs, act, upf, outf, g2p, g2s, gate, g1, d2, d1,
):
    low[...], high[...] = ends_of(side[0] == 1, inner_x, outer_x)
    low_ends[...], high_ends[...] = ends_of(side[0] == 1, inner, outer)
    fh, mh = FIELD_HALO, MASK_HALO
    ex, ey, uy = cx + 2 * fh, cy + 2 * fh, cy + 2
    nf, nu = cx * fh * kz, cx * 2 * kz
    nx, nw = fh * cy * kz, cy * 2 * kz
    ne, nv = fh * 2 * fh * kz, 2 * kz
    xp[fh : fh + cx, fh : fh + cy] = field[...]
    xp[fh : fh + cx, 0:fh] = left[0:nf].reshape(cx, fh, kz, LANES)
    xp[fh : fh + cx, fh + cy :] = right[0:nf].reshape(cx, fh, kz, LANES)
    for at, own, ends in ((0, low, low_ends), (fh + cx, high, high_ends)):
        xp[at : at + fh, fh : fh + cy] = own[0:nx].reshape(fh, cy, kz, LANES)
        block = ends[0:ne].reshape(fh, 2 * fh, kz, LANES)
        xp[at : at + fh, 0:fh] = block[:, :fh]
        xp[at : at + fh, fh + cy :] = block[:, fh:]

    def fill_side(i):
        rows = xp[i].reshape(ey * kz, LANES).astype(F32)
        depth = lax.rem(lax.broadcasted_iota(jnp.int32, rows.shape, 0), kz)
        lane = lax.broadcasted_iota(jnp.int32, rows.shape, 1)
        above = jnp.where(depth == kz - 1, 0.0, pltpu.roll(rows, ey * kz - 1, 0))
        below = jnp.where(depth == 0, 0.0, pltpu.roll(rows, 1, 0))
        both = jnp.where(lane < LANES // 2, above, below).astype(BF)
        xs[i] = both.reshape(ey, kz, LANES)
    for i in range(ex):
        fill_side(i)
    span = uy * 2 * kz

    def put_up(x, y, cols, value):
        base = x * span + y * 2 * kz
        upf[base : base + cols * 2 * kz] = value.reshape(-1, LANES).astype(F32)

    for x, own, ends in ((0, low, low_ends), (cx + 1, high, high_ends)):
        put_up(x, 1, cy, own[nx : nx + nw])
        put_up(x, 0, 1, ends[ne : ne + nv])
        put_up(x, cy + 1, 1, ends[ne + nv : ne + 2 * nv])
    for x in range(cx):
        at = nf + x * 2 * kz
        put_up(x + 1, 0, 1, left[at : at + 2 * kz])
        put_up(x + 1, 1, cy, up[x])
        put_up(x + 1, cy + 1, 1, right[at : at + 2 * kz])

    def put_mask(source, sx, sy, x, y):
        for parity in range(2):
            lane = sx * cy + sy + parity * (LANES // 2)
            value = jnp.broadcast_to(source[:, lane : lane + 1], (kz, LANES))
            act[x, y, :, parity * LANES : (parity + 1) * LANES] = value.astype(BF)

    def three(ends, own):
        at = ne + 2 * nv
        rows = ends[at : at + kz], own[nx + nw :], ends[at + kz :]
        return [part.astype(F32) for part in rows]

    rows_mid = [left[nf + nu :].astype(F32), tile[...].astype(F32), right[nf + nu :].astype(F32)]
    rows_low, rows_high = three(low_ends, low), three(high_ends, high)
    for x in range(cx + 2 * mh):
        if x < mh:
            sources, sx = rows_low, cx - mh + x
        elif x < mh + cx:
            sources, sx = rows_mid, x - mh
        else:
            sources, sx = rows_high, x - mh - cx
        for y in range(cy):
            put_mask(sources[1], sx, y, x, mh + y)
        for j in range(mh):
            put_mask(sources[0], sx, cy - mh + j, x, j)
            put_mask(sources[2], sx, j, x, mh + cy + j)

    bias1 = jnp.concatenate([b1[...], b1[...]], axis=1)
    bias2 = jnp.concatenate([b2[...], b2[...]], axis=1)

    hx, hy = cx + 4, cy + 4
    step = 1

    def first(i):
        at = i * step
        window = taps_of(xp, xs, at, step, hy)
        z = jnp.dot(window, w1[...], preferred_element_type=F32) + bias1
        s = jax.nn.sigmoid(z)
        m = act[pl.ds(at, step)].reshape(step * hy * kz, 2 * LANES).astype(F32)
        h = z * s * m
        above, below = side_pair(h, kz, LANES)
        hp[pl.ds(at, step)] = h.astype(BF).reshape(step, hy, kz, 2 * LANES)
        both = jnp.concatenate([above, below], axis=1).astype(BF)
        hs[pl.ds(at, step)] = both.reshape(step, hy, kz, 2 * LANES)

        if 2 // step <= i < (2 + cx) // step:
            factor = m * s * (1.0 + z * (1.0 - s))
            factor = factor.reshape(step, hy, kz, 2 * LANES)[:, 2 : 2 + cy]
            gate[pl.ds(at - 2, step)] = factor

    for i in range(hx // step):
        first(i)

    def second(i):
        at = i * step
        window = taps_of(hp, hs, at, step, uy)
        z = jnp.dot(window, w2[...], preferred_element_type=F32) + bias2
        s = jax.nn.sigmoid(z)
        m = act[pl.ds(at + 1, step), 1 : 1 + uy].reshape(-1, 2 * LANES).astype(F32)
        rows = step * uy * kz
        base = at * span
        u = jnp.concatenate(
            [upf[pl.ds(base, rows, stride=2), :], upf[pl.ds(base + 1, rows, stride=2), :]], axis=1
        )
        g = u * m * s * (1.0 + z * (1.0 - s))
        gb = g.astype(BF)
        above, below = side_pair(g, kz, LANES)
        g2p[pl.ds(at, step)] = gb.reshape(step, uy, kz, 2 * LANES)
        both = jnp.concatenate([above, below], axis=1).astype(BF)
        g2s[pl.ds(at, step)] = both.reshape(step, uy, kz, 2 * LANES)
        out = z * s * m
        outf[pl.ds(base, rows, stride=2), :] = out[:, :LANES]
        outf[pl.ds(base + 1, rows, stride=2), :] = out[:, LANES:]
    for i in range((cx + 2) // step):
        second(i)
    for x in range(cx):
        base = (x + 1) * span + 2 * kz
        rows = outf[base : base + cy * 2 * kz].astype(BF)
        features[x] = rows.reshape(cy, 2 * kz, LANES)

    own = hp[2 : 2 + cx, 2 : 2 + cy].reshape(-1, 2 * LANES)
    turned = own.T
    for a in range(3):
        for b in range(3):
            parts = [
                ref[2 - a : 2 - a + cx, 2 - b : 2 - b + cy].reshape(-1, 2 * LANES)
                for ref in (g2p, g2s)
            ]
            for half, part in enumerate(parts):
                block = jnp.dot(turned, part, preferred_element_type=F32)
                q = [[block[r * LANES : (r + 1) * LANES, c * LANES : (c + 1) * LANES] for c in (0, 1)] for r in (0, 1)]
                t = 9 * a + 3 * b
                if half == 0:
                    d2[t + 1] = q[0][0] + q[1][1]
                    d2[t] = q[0][1]
                    d2[t + 2] = q[1][0]
                else:
                    d2[t] = d2[t] + q[1][0]
                    d2[t + 2] = d2[t + 2] + q[0][1]

    rows = step * cy * kz

    def grad(i):
        at = i * step
        window = taps_of(g2p, g2s, at, step, cy)
        e = jnp.dot(window, w3[...], preferred_element_type=F32)
        g = e * gate[pl.ds(at, step)].reshape(rows, 2 * LANES)
        g1[i * rows : (i + 1) * rows] = g.astype(BF)
    for i in range(cx // step):
        grad(i)
    right_side = g1[...]
    cells = cx * cy * kz
    half = LANES // 2
    for b in range(3):
        cols = slice(fh - 1 + b, fh - 1 + b + cy)
        parts = [ref[fh - 1 : fh + 1 + cx, cols].reshape(-1, LANES) for ref in (xp, xs)]
        turned = jnp.concatenate(parts, axis=1).T
        for a in range(3):
            at = a * cy * kz
            block = jnp.dot(turned[:, at : at + cells], right_side, preferred_element_type=F32)
            q = [
                [block[r * half : (r + 1) * half, c * LANES : (c + 1) * LANES] for c in (0, 1)]
                for r in range(4)
            ]
            t = 9 * a + 3 * b
            d1[t] = q[0][1] + q[3][0]
            d1[t + 1] = q[0][0] + q[1][1]
            d1[t + 2] = q[1][0] + q[2][1]
    at = 0
    for total in (d2, d1):
        half = total.shape[1] // 2
        mine = pl.multiple_of(side[0] * half, half)
        other = pl.multiple_of((1 - side[0]) * half, half)
        sent[:, at : at + half] = total[:, pl.ds(other, half)].astype(BF)
        kept[:, at : at + half] = total[:, pl.ds(mine, half)]
        at += half


def norm_body(side, own_a, own_b, other_a, other_b, out2, out1, held2, held1, sems):
    taps = out2.shape[0]
    split = own_a.shape[0]
    rows_of = held2.shape[1] // 2, held1.shape[1] // 2
    stride = sum(rows_of)

    def rows(pair, start, count):
        low, high = pair
        parts = []
        if start < split:
            parts.append(low[start : min(start + count, split)])
        if start + count > split:
            parts.append(high[max(start, split) - split : start + count - split])
        return jnp.concatenate(parts, axis=0).astype(F32)

    def spans():
        for t in range(taps):
            for i, at in ((0, t * stride), (1, t * stride + rows_of[0])):
                yield t, i, at

    squares = [jnp.zeros((8, LANES), F32), jnp.zeros((8, LANES), F32)]
    for t, i, at in spans():
        for pair in ((own_a, own_b), (other_a, other_b)):
            value = rows(pair, at, rows_of[i])
            squares[i] += jnp.sum((value * value).reshape(-1, 8, LANES), axis=0)
    scales = [
        lax.rsqrt(jnp.full((1, LANES), jnp.sum(total)) / float(out.size) + 1e-06)
        for total, out in zip(squares, (out2, out1))
    ]
    group = taps // 3
    copies = []
    for t, i, at in spans():
        held, count = (held2, held1)[i], rows_of[i]
        mine = pl.multiple_of(side[0] * count, count)
        rest = pl.multiple_of((1 - side[0]) * count, count)
        held[t, pl.ds(mine, count)] = rows((own_a, own_b), at, count) * scales[i]
        held[t, pl.ds(rest, count)] = rows((other_a, other_b), at, count) * scales[i]
        if i == 1 and (t + 1) % group == 0:
            span = pl.ds(t + 1 - group, group)
            for held, out in ((held2, out2), (held1, out1)):
                copy = pltpu.make_async_copy(held.at[span], out.at[span], sems.at[len(copies)])
                copy.start()
                copies.append(copy)
    for copy in copies:
        copy.wait()


PAIR_TAPS = ((1, 0), (2, 1), (None, 2), (0, None))


def weights_body(first, second, _, w1, w2, w3):
    taps = second.shape[0]

    def group(g, carry):
        for source, out, turn in ((first, w1, False), (second, w2, False), (second, w3, True)):
            depth, width = source.shape[1:]
            if turn:
                block = [source[taps - 1 - 3 * g - c].astype(F32).T.astype(BF) for c in range(3)]
            else:
                block = [source[3 * g + c] for c in range(3)]
            none = jnp.zeros((depth, width), BF)
            for r, row in enumerate(PAIR_TAPS):
                at = pl.multiple_of(g * 4 * depth + r * depth, depth)
                for c, tap in enumerate(row):
                    value = none if tap is None else block[tap]
                    out[pl.ds(at, depth), c * width : (c + 1) * width] = value
        return carry

    lax.fori_loop(0, taps // 3, group, 0)


def local_call(body, name, out, scratch=(), scalars=0, in_hbm=(), out_hbm=(), limit=24):
    def call(*args):
        vmem = pl.BlockSpec(memory_space=pltpu.VMEM)
        hbm = pl.BlockSpec(memory_space=pltpu.HBM)
        ins = [
            pl.BlockSpec(memory_space=pltpu.SMEM) if i < scalars else hbm if i in in_hbm else vmem
            for i in range(len(args))
        ]
        held = [
            a
            if i < scalars
            else pltpu.with_memory_space_constraint(a, pltpu.HBM if i in in_hbm else pltpu.VMEM)
            for i, a in enumerate(args)
        ]
        outs = [
            (pltpu.HBM if i in out_hbm else pltpu.VMEM)(o.shape, o.dtype) for i, o in enumerate(out)
        ]
        return pl.pallas_call(
            body,
            out_shape=outs,
            in_specs=ins,
            out_specs=[hbm if i in out_hbm else vmem for i in range(len(out))],
            scratch_shapes=list(scratch),
            compiler_params=pltpu.CompilerParams(vmem_limit_bytes=limit << 20),
            name=name,
        )(*held)

    return call


def on_device(volume, basin_mask, w_first, b_first, w_second, b_second, upstream):
    cx, cy, kz, _ = volume.shape
    taps, _, chan = w_first.shape
    part = functools.partial
    shape = jax.ShapeDtypeStruct
    levels = bit_levels(("gx", "gy"))
    core = levels[0]
    side = side_of(core).astype(jnp.int32).reshape(1)
    odd_y = side_of(("gy", 1)).astype(jnp.int32).reshape(1)
    ex, ey, uy = cx + 2 * FIELD_HALO, cy + 2 * FIELD_HALO, cy + 2
    rows_y = cx * FIELD_HALO * kz + cx * 2 * kz + kz
    rows_x = FIELD_HALO * cy * kz + cy * 2 * kz + kz
    rows_e = FIELD_HALO * 2 * FIELD_HALO * kz + 2 * 2 * kz + 2 * kz
    inner_y, outer_y, inner_x, outer_x, tile, field, up, w_one, w_two = local_call(
        part(pack_own_body, cx, cy, kz),
        "pack_own",
        [shape((rows_y, LANES), BF)] * 2
        + [shape((rows_x, LANES), BF)] * 2
        + [shape((kz, LANES), BF)]
        + [shape(a.shape, BF) for a in (volume, upstream, w_first, w_second)],
        [pltpu.VMEM(basin_mask.shape, jnp.int32)]
        + [pltpu.VMEM((LANES, LANES), F32)] * 2
        + [pltpu.SemaphoreType.DMA((5,))],
        scalars=2,
        in_hbm=(2, 3, 4, 5, 6),
    )(side, odd_y, volume, upstream, basin_mask, w_first, w_second)
    inner_y, outer_y = exchange(inner_y, outer_y, "gy")
    inner_x, outer_x = exchange(inner_x, outer_x, "gx")
    inner, outer, left, right = local_call(
        part(pack_corner_body, cx, cy, kz),
        "pack_corner",
        [shape((rows_e, LANES), BF)] * 2 + [shape((rows_y, LANES), BF)] * 2,
        scalars=2,
    )(side, odd_y, inner_y, outer_y)
    corner = inner
    inner, outer = exchange(inner, outer, "gx")
    w1, w2, w3 = local_call(
        weights_body,
        "weights",
        [
            shape((4 * taps // 3 * w_first.shape[1], 2 * chan), BF),
            shape((4 * taps // 3 * chan, 2 * chan), BF),
            shape((4 * taps // 3 * chan, 2 * chan), BF),
        ],
    )(w_one, w_two, corner)
    rows = chan // 2 + w_first.shape[1] // 2
    pairs = (kz, 2 * chan)
    features, sent, kept = local_call(
        part(compute_body, cx, cy, kz),
        "compute",
        [
            shape((cx, cy, 2 * kz, chan), BF),
            shape((taps, rows, chan), BF),
            shape((taps, rows, chan), F32),
        ],
        [pltpu.VMEM((rows_x, LANES), BF)] * 2
        + [pltpu.VMEM((rows_e, LANES), BF)] * 2
        + [
            pltpu.VMEM((ex, ey, kz, LANES), BF),
            pltpu.VMEM((ex, ey, kz, LANES), BF),
            pltpu.VMEM((cx + 4, cy + 4, *pairs), BF),
            pltpu.VMEM((cx + 4, cy + 4, *pairs), BF),
            pltpu.VMEM((cx + 4, cy + 4, *pairs), BF),
            pltpu.VMEM(((cx + 2) * uy * 2 * kz, LANES), F32),
            pltpu.VMEM(((cx + 2) * uy * 2 * kz, LANES), F32),
            pltpu.VMEM((cx + 2, uy, *pairs), BF),
            pltpu.VMEM((cx + 2, uy, *pairs), BF),
            pltpu.VMEM((cx, cy, *pairs), F32),
            pltpu.VMEM((cx * cy * kz, 2 * chan), BF),
            pltpu.VMEM(w_second.shape, F32),
            pltpu.VMEM(w_first.shape, F32),
        ],
        scalars=1,
        limit=32,
    )(side, field, up, tile, left, right, inner_x, outer_x, inner, outer, w1, b_first.reshape(1, -1), w2, b_second.reshape(1, -1), w3)
    total = kept.reshape(-1, chan) + swap(sent.reshape(-1, chan), core).astype(F32)
    own = summed_everywhere(total, levels[1:])
    other = [swap(part_of, core) for part_of in own]
    step_second, step_first = local_call(
        norm_body,
        "normalize",
        [shape(w_second.shape, F32), shape(w_first.shape, F32)],
        [
            pltpu.VMEM(w_second.shape, F32),
            pltpu.VMEM(w_first.shape, F32),
            pltpu.SemaphoreType.DMA((6,)),
        ],
        scalars=1,
        out_hbm=(0, 1),
    )(side, *own, *other)
    return (features, step_first, step_second)


def solution(mesh):
    in_specs = (
        P("gx", "gy", None, None),
        P("gx", "gy", None),
        P(),
        P(),
        P(),
        P(),
        P("gx", "gy", None, None),
    )
    out_specs = (P("gx", "gy", None, None), P(), P())
    return jax.shard_map(
        on_device, mesh=mesh, in_specs=in_specs, out_specs=out_specs, check_vma=False
    )
```

```python
import functools

import jax
import jax.numpy as jnp
from jax import lax
from jax.experimental import pallas as pl
from jax.experimental.pallas import tpu as pltpu
from jax.sharding import PartitionSpec as P

BF = jnp.bfloat16
F32 = jnp.float32
LANES = 128
FIELD_HALO = 3
MASK_HALO = 2


def bit_levels(axes):
    levels = []
    for axis in axes:
        bit = 1
        while bit < lax.axis_size(axis):
            levels.append((axis, bit))
            bit *= 2
    return levels


def swap(part, level):
    axis, bit = level
    return lax.ppermute(part, axis, [(i, i ^ bit) for i in range(lax.axis_size(axis))])


def side_of(level):
    axis, bit = level
    return lax.rem(lax.axis_index(axis) // bit, 2)


def halves(part, level):
    half = part.shape[0] // 2
    side = side_of(level)
    sent = lax.dynamic_slice_in_dim(part, (1 - side) * half, half, 0).astype(BF)
    kept = lax.dynamic_slice_in_dim(part, side * half, half, 0)
    return sent, kept


def joined(own, other, level):
    return jnp.where(
        side_of(level) == 0,
        jnp.concatenate([own, other], axis=0),
        jnp.concatenate([other, own], axis=0),
    )


def summed_everywhere(total, levels):
    one, two, middle, final = levels[0], levels[1], levels[2:-1], levels[-1]
    parts = total
    for order in ((one, two), (two, one)):
        split = [halves(part, level) for part, level in zip(parts, order)]
        got = [swap(sent, level) for (sent, _), level in zip(split, order)]
        parts = [kept + other.astype(F32) for (_, kept), other in zip(split, got)]
    both = jnp.concatenate(parts, axis=0)
    for level in middle:
        sent, kept = halves(both, level)
        both = kept + swap(sent, level).astype(F32)
    both = both.astype(BF)
    both = (both.astype(F32) + swap(both, final).astype(F32)).astype(BF)
    for level in reversed(middle):
        both = joined(both, swap(both, level), level)
    cut = both.shape[0] // 2
    parts = [both[:cut], both[cut:]]
    for order in ((two, one), (one, two)):
        got = [swap(part, level) for part, level in zip(parts, order)]
        parts = [joined(own, other, level) for own, other, level in zip(parts, got, order)]
    return parts


def exchange(inner, outer, axis):
    count = lax.axis_size(axis)
    pairs = [(i, i + 1) for i in range(1, count - 1, 2)]
    outer = lax.ppermute(outer, axis, pairs + [(b, a) for a, b in pairs])
    inner = lax.ppermute(inner, axis, [(i, i ^ 1) for i in range(count)])
    return inner, outer


def ends_of(odd, inner, outer):
    first, second = inner[...], outer[...]
    return jnp.where(odd, first, second), jnp.where(odd, second, first)


def put_rows(ref, parts):
    row = 0
    for part in parts:
        rows = part.reshape(-1, LANES)
        ref[row : row + rows.shape[0]] = rows
        row += rows.shape[0]


def pack_own_body(
    cx, cy, kz, odd, odd_y, hfield, hup, hmask,
    inner_y, outer_y, inner_x, outer_x, tile, field, up,
    mask, square, deep, sems,
):
    fh = FIELD_HALO
    pairs = (
        (hmask, mask),
        (hfield, field),
        (hup, up),
    )
    copies = [
        pltpu.make_async_copy(source, target, sems.at[i])
        for i, (source, target) in enumerate(pairs)
    ]
    for copy in copies:
        copy.start()
    cells = cx * cy
    square[...] = jnp.zeros_like(square)
    copies[0].wait()
    square[0:cells, 0 : 2 * kz] = mask[...].reshape(cells, 2 * kz).astype(F32)
    deep[...] = square[...].T
    at_even = deep[pl.ds(0, kz, stride=2), :]
    at_odd = deep[pl.ds(1, kz, stride=2), :]
    tile[...] = (at_even + pltpu.roll(at_odd, LANES // 2, 1)).astype(BF)
    copies[1].wait()
    copies[2].wait()
    for ref, end in ((inner_y, 1 - odd_y[0]), (outer_y, odd_y[0])):
        put_rows(
            ref,
            (field[:, pl.ds(end * (cy - fh), fh)], up[:, pl.ds(end * (cy - 1), 1)], tile[...]),
        )
    for ref, end in ((inner_x, 1 - odd[0]), (outer_x, odd[0])):
        put_rows(
            ref, (field[pl.ds(end * (cx - fh), fh)], up[pl.ds(end * (cx - 1), 1)], tile[...])
        )


def pack_corner_body(cx, cy, kz, odd, odd_y, inner_y, outer_y, inner, outer, left, right):
    left[...], right[...] = ends_of(odd_y[0] == 1, inner_y, outer_y)
    fh = FIELD_HALO
    nf, nu = cx * fh * kz, cx * 2 * kz
    for ref, end in ((inner, 1 - odd[0]), (outer, odd[0])):
        parts = []
        for r in range(fh):
            at = pl.multiple_of((end * (cx - fh) + r) * fh * kz, kz)
            parts += [left[pl.ds(at, fh * kz)], right[pl.ds(at, fh * kz)]]
        at = pl.multiple_of(nf + end * (cx - 1) * 2 * kz, kz)
        parts += [left[pl.ds(at, 2 * kz)], right[pl.ds(at, 2 * kz)]]
        parts += [left[nf + nu :], right[nf + nu :]]
        put_rows(ref, parts)


def side_pair(pair, kz, width):
    rows = pair.shape[0]
    depth = lax.rem(lax.broadcasted_iota(jnp.int32, (rows, width), 0), kz)
    above = pltpu.roll(pair[:, :width], rows - 1, 0)
    below = pltpu.roll(pair[:, width:], 1, 0)
    above = jnp.where(depth == kz - 1, 0.0, above)
    below = jnp.where(depth == 0, 0.0, below)
    return above, below


def taps_of(pair, side, at, rows, cols):
    parts = []
    for a in range(3):
        for b in range(3):
            for ref in (pair, side):
                part = ref[pl.ds(at + a, rows), b : b + cols]
                parts.append(part.reshape(-1, part.shape[-1]))
    return jnp.concatenate(parts, axis=1)


def compute_body(
    cx, cy, kz,
    side, field, up, tile, left, right, inner_x, outer_x, inner, outer, w1, b1, w2, b2, w3,
    features, sent, kept,
    low, high, low_ends, high_ends,
    xp, xs, hp, hs, act, upf, outf, g2p, g2s, gate, g1, d2, d1, shown, sem,
):
    low[...], high[...] = ends_of(side[0] == 1, inner_x, outer_x)
    low_ends[...], high_ends[...] = ends_of(side[0] == 1, inner, outer)
    fh, mh = FIELD_HALO, MASK_HALO
    ex, ey, uy = cx + 2 * fh, cy + 2 * fh, cy + 2
    nf, nu = cx * fh * kz, cx * 2 * kz
    nx, nw = fh * cy * kz, cy * 2 * kz
    ne, nv = fh * 2 * fh * kz, 2 * kz
    xp[fh : fh + cx, fh : fh + cy] = field[...]
    xp[fh : fh + cx, 0:fh] = left[0:nf].reshape(cx, fh, kz, LANES)
    xp[fh : fh + cx, fh + cy :] = right[0:nf].reshape(cx, fh, kz, LANES)
    for at, own, ends in ((0, low, low_ends), (fh + cx, high, high_ends)):
        xp[at : at + fh, fh : fh + cy] = own[0:nx].reshape(fh, cy, kz, LANES)
        block = ends[0:ne].reshape(fh, 2 * fh, kz, LANES)
        xp[at : at + fh, 0:fh] = block[:, :fh]
        xp[at : at + fh, fh + cy :] = block[:, fh:]

    def fill_side(i):
        rows = xp[i].reshape(ey * kz, LANES).astype(F32)
        depth = lax.rem(lax.broadcasted_iota(jnp.int32, rows.shape, 0), kz)
        lane = lax.broadcasted_iota(jnp.int32, rows.shape, 1)
        above = jnp.where(depth == kz - 1, 0.0, pltpu.roll(rows, ey * kz - 1, 0))
        below = jnp.where(depth == 0, 0.0, pltpu.roll(rows, 1, 0))
        both = jnp.where(lane < LANES // 2, above, below).astype(BF)
        xs[i] = both.reshape(ey, kz, LANES)
    for i in range(ex):
        fill_side(i)
    span = uy * 2 * kz

    def put_up(x, y, cols, value):
        base = x * span + y * 2 * kz
        upf[base : base + cols * 2 * kz] = value.reshape(-1, LANES).astype(F32)

    for x, own, ends in ((0, low, low_ends), (cx + 1, high, high_ends)):
        put_up(x, 1, cy, own[nx : nx + nw])
        put_up(x, 0, 1, ends[ne : ne + nv])
        put_up(x, cy + 1, 1, ends[ne + nv : ne + 2 * nv])
    for x in range(cx):
        at = nf + x * 2 * kz
        put_up(x + 1, 0, 1, left[at : at + 2 * kz])
        put_up(x + 1, 1, cy, up[x])
        put_up(x + 1, cy + 1, 1, right[at : at + 2 * kz])

    def put_mask(source, sx, sy, x, y):
        for parity in range(2):
            lane = sx * cy + sy + parity * (LANES // 2)
            value = jnp.broadcast_to(source[:, lane : lane + 1], (kz, LANES))
            act[x, y, :, parity * LANES : (parity + 1) * LANES] = value.astype(BF)

    def three(ends, own):
        at = ne + 2 * nv
        rows = ends[at : at + kz], own[nx + nw :], ends[at + kz :]
        return [part.astype(F32) for part in rows]

    rows_mid = [left[nf + nu :].astype(F32), tile[...].astype(F32), right[nf + nu :].astype(F32)]
    rows_low, rows_high = three(low_ends, low), three(high_ends, high)
    for x in range(cx + 2 * mh):
        if x < mh:
            sources, sx = rows_low, cx - mh + x
        elif x < mh + cx:
            sources, sx = rows_mid, x - mh
        else:
            sources, sx = rows_high, x - mh - cx
        for y in range(cy):
            put_mask(sources[1], sx, y, x, mh + y)
        for j in range(mh):
            put_mask(sources[0], sx, cy - mh + j, x, j)
            put_mask(sources[2], sx, j, x, mh + cy + j)

    bias1 = jnp.concatenate([b1[...], b1[...]], axis=1)
    bias2 = jnp.concatenate([b2[...], b2[...]], axis=1)

    hx, hy = cx + 4, cy + 4
    step = 1

    def first(i):
        at = i * step
        window = taps_of(xp, xs, at, step, hy)
        z = jnp.dot(window, w1[...], preferred_element_type=F32) + bias1
        s = jax.nn.sigmoid(z)
        m = act[pl.ds(at, step)].reshape(step * hy * kz, 2 * LANES).astype(F32)
        h = z * s * m
        above, below = side_pair(h, kz, LANES)
        hp[pl.ds(at, step)] = h.astype(BF).reshape(step, hy, kz, 2 * LANES)
        both = jnp.concatenate([above, below], axis=1).astype(BF)
        hs[pl.ds(at, step)] = both.reshape(step, hy, kz, 2 * LANES)

        if 2 // step <= i < (2 + cx) // step:
            factor = m * s * (1.0 + z * (1.0 - s))
            factor = factor.reshape(step, hy, kz, 2 * LANES)[:, 2 : 2 + cy]
            gate[pl.ds(at - 2, step)] = factor

    for i in range(hx // step):
        first(i)

    def second(i):
        at = i * step
        window = taps_of(hp, hs, at, step, uy)
        z = jnp.dot(window, w2[...], preferred_element_type=F32) + bias2
        s = jax.nn.sigmoid(z)
        m = act[pl.ds(at + 1, step), 1 : 1 + uy].reshape(-1, 2 * LANES).astype(F32)
        rows = step * uy * kz
        base = at * span
        u = jnp.concatenate(
            [upf[pl.ds(base, rows, stride=2), :], upf[pl.ds(base + 1, rows, stride=2), :]], axis=1
        )
        g = u * m * s * (1.0 + z * (1.0 - s))
        gb = g.astype(BF)
        above, below = side_pair(g, kz, LANES)
        g2p[pl.ds(at, step)] = gb.reshape(step, uy, kz, 2 * LANES)
        both = jnp.concatenate([above, below], axis=1).astype(BF)
        g2s[pl.ds(at, step)] = both.reshape(step, uy, kz, 2 * LANES)
        out = z * s * m
        outf[pl.ds(base, rows, stride=2), :] = out[:, :LANES]
        outf[pl.ds(base + 1, rows, stride=2), :] = out[:, LANES:]
    for i in range((cx + 2) // step):
        second(i)
    for x in range(cx):
        base = (x + 1) * span + 2 * kz
        rows = outf[base : base + cy * 2 * kz].astype(BF)
        shown[x] = rows.reshape(cy, 2 * kz, LANES)
    show = pltpu.make_async_copy(shown, features, sem)
    show.start()

    own = hp[2 : 2 + cx, 2 : 2 + cy].reshape(-1, 2 * LANES)
    turned = own.T
    for a in range(3):
        for b in range(3):
            parts = [
                ref[2 - a : 2 - a + cx, 2 - b : 2 - b + cy].reshape(-1, 2 * LANES)
                for ref in (g2p, g2s)
            ]
            for half, part in enumerate(parts):
                block = jnp.dot(turned, part, preferred_element_type=F32)
                q = [[block[r * LANES : (r + 1) * LANES, c * LANES : (c + 1) * LANES] for c in (0, 1)] for r in (0, 1)]
                t = 9 * a + 3 * b
                if half == 0:
                    d2[t + 1] = q[0][0] + q[1][1]
                    d2[t] = q[0][1]
                    d2[t + 2] = q[1][0]
                else:
                    d2[t] = d2[t] + q[1][0]
                    d2[t + 2] = d2[t + 2] + q[0][1]

    rows = step * cy * kz

    def grad(i):
        at = i * step
        window = taps_of(g2p, g2s, at, step, cy)
        e = jnp.dot(window, w3[...], preferred_element_type=F32)
        g = e * gate[pl.ds(at, step)].reshape(rows, 2 * LANES)
        g1[i * rows : (i + 1) * rows] = g.astype(BF)
    for i in range(cx // step):
        grad(i)
    right_side = g1[...]
    cells = cx * cy * kz
    half = LANES // 2
    for b in range(3):
        cols = slice(fh - 1 + b, fh - 1 + b + cy)
        parts = [ref[fh - 1 : fh + 1 + cx, cols].reshape(-1, LANES) for ref in (xp, xs)]
        turned = jnp.concatenate(parts, axis=1).T
        for a in range(3):
            at = a * cy * kz
            block = jnp.dot(turned[:, at : at + cells], right_side, preferred_element_type=F32)
            q = [
                [block[r * half : (r + 1) * half, c * LANES : (c + 1) * LANES] for c in (0, 1)]
                for r in range(4)
            ]
            t = 9 * a + 3 * b
            d1[t] = q[0][1] + q[3][0]
            d1[t + 1] = q[0][0] + q[1][1]
            d1[t + 2] = q[1][0] + q[2][1]
    at = 0
    for total in (d2, d1):
        half = total.shape[1] // 2
        mine = pl.multiple_of(side[0] * half, half)
        other = pl.multiple_of((1 - side[0]) * half, half)
        sent[:, at : at + half] = total[:, pl.ds(other, half)].astype(BF)
        kept[:, at : at + half] = total[:, pl.ds(mine, half)]
        at += half
    show.wait()


def norm_body(side, own_a, own_b, other_a, other_b, out2, out1, held2, held1, sems):
    taps = out2.shape[0]
    split = own_a.shape[0]
    rows_of = held2.shape[1] // 2, held1.shape[1] // 2
    stride = sum(rows_of)

    def rows(pair, start, count):
        low, high = pair
        parts = []
        if start < split:
            parts.append(low[start : min(start + count, split)])
        if start + count > split:
            parts.append(high[max(start, split) - split : start + count - split])
        return jnp.concatenate(parts, axis=0).astype(F32)

    def spans():
        for t in range(taps):
            for i, at in ((0, t * stride), (1, t * stride + rows_of[0])):
                yield t, i, at

    squares = [jnp.zeros((8, LANES), F32), jnp.zeros((8, LANES), F32)]
    for t, i, at in spans():
        for pair in ((own_a, own_b), (other_a, other_b)):
            value = rows(pair, at, rows_of[i])
            squares[i] += jnp.sum((value * value).reshape(-1, 8, LANES), axis=0)
    scales = [
        lax.rsqrt(jnp.full((1, LANES), jnp.sum(total)) / float(out.size) + 1e-06)
        for total, out in zip(squares, (out2, out1))
    ]
    group = taps // 9
    copies = []
    for t, i, at in spans():
        held, count = (held2, held1)[i], rows_of[i]
        mine = pl.multiple_of(side[0] * count, count)
        rest = pl.multiple_of((1 - side[0]) * count, count)
        held[t, pl.ds(mine, count)] = rows((own_a, own_b), at, count) * scales[i]
        held[t, pl.ds(rest, count)] = rows((other_a, other_b), at, count) * scales[i]
        if i == 1 and (t + 1) % group == 0:
            span = pl.ds(t + 1 - group, group)
            for held, out in ((held2, out2), (held1, out1)):
                copy = pltpu.make_async_copy(held.at[span], out.at[span], sems.at[len(copies)])
                copy.start()
                copies.append(copy)
    for copy in copies:
        copy.wait()


PAIR_TAPS = ((1, 0), (2, 1), (None, 2), (0, None))


def weights_body(hfirst, hsecond, _, w1, w2, w3, first, second, sems):
    taps = second.shape[0]
    copies = [
        pltpu.make_async_copy(hfirst, first, sems.at[0]),
        pltpu.make_async_copy(hsecond, second, sems.at[1]),
    ]
    for copy in copies:
        copy.start()

    def group(g, kinds):
        for source, out, turn in kinds:
            depth, width = source.shape[1:]
            if turn:
                block = [source[taps - 1 - 3 * g - c].astype(F32).T.astype(BF) for c in range(3)]
            else:
                block = [source[3 * g + c] for c in range(3)]
            none = jnp.zeros((depth, width), BF)
            for r, row in enumerate(PAIR_TAPS):
                at = pl.multiple_of(g * 4 * depth + r * depth, depth)
                for c, tap in enumerate(row):
                    value = none if tap is None else block[tap]
                    out[pl.ds(at, depth), c * width : (c + 1) * width] = value

    for copy, kinds in zip(copies, (((first, w1, False),), ((second, w2, False), (second, w3, True)))):
        copy.wait()

        @pl.loop(0, taps // 3)
        def _(g):
            group(g, kinds)


def local_call(body, name, out, scratch=(), scalars=0, in_hbm=(), out_hbm=(), limit=24):
    def call(*args):
        vmem = pl.BlockSpec(memory_space=pltpu.VMEM)
        hbm = pl.BlockSpec(memory_space=pltpu.HBM)
        ins = [
            pl.BlockSpec(memory_space=pltpu.SMEM) if i < scalars else hbm if i in in_hbm else vmem
            for i in range(len(args))
        ]
        held = [
            a
            if i < scalars
            else pltpu.with_memory_space_constraint(a, pltpu.HBM if i in in_hbm else pltpu.VMEM)
            for i, a in enumerate(args)
        ]
        outs = [
            (pltpu.HBM if i in out_hbm else pltpu.VMEM)(o.shape, o.dtype) for i, o in enumerate(out)
        ]
        return pl.pallas_call(
            body,
            out_shape=outs,
            in_specs=ins,
            out_specs=[hbm if i in out_hbm else vmem for i in range(len(out))],
            scratch_shapes=list(scratch),
            compiler_params=pltpu.CompilerParams(vmem_limit_bytes=limit << 20),
            name=name,
        )(*held)

    return call


def on_device(volume, basin_mask, w_first, b_first, w_second, b_second, upstream):
    cx, cy, kz, _ = volume.shape
    taps, _, chan = w_first.shape
    part = functools.partial
    shape = jax.ShapeDtypeStruct
    levels = bit_levels(("gx", "gy"))
    core = levels[0]
    side = side_of(core).astype(jnp.int32).reshape(1)
    odd_y = side_of(("gy", 1)).astype(jnp.int32).reshape(1)
    ex, ey, uy = cx + 2 * FIELD_HALO, cy + 2 * FIELD_HALO, cy + 2
    rows_y = cx * FIELD_HALO * kz + cx * 2 * kz + kz
    rows_x = FIELD_HALO * cy * kz + cy * 2 * kz + kz
    rows_e = FIELD_HALO * 2 * FIELD_HALO * kz + 2 * 2 * kz + 2 * kz
    inner_y, outer_y, inner_x, outer_x, tile, field, up = local_call(
        part(pack_own_body, cx, cy, kz),
        "pack_own",
        [shape((rows_y, LANES), BF)] * 2
        + [shape((rows_x, LANES), BF)] * 2
        + [shape((kz, LANES), BF)]
        + [shape(a.shape, BF) for a in (volume, upstream)],
        [pltpu.VMEM(basin_mask.shape, jnp.int32)]
        + [pltpu.VMEM((LANES, LANES), F32)] * 2
        + [pltpu.SemaphoreType.DMA((3,))],
        scalars=2,
        in_hbm=(2, 3, 4),
    )(side, odd_y, volume, upstream, basin_mask)
    inner_y, outer_y = exchange(inner_y, outer_y, "gy")
    inner_x, outer_x = exchange(inner_x, outer_x, "gx")
    inner, outer, left, right = local_call(
        part(pack_corner_body, cx, cy, kz),
        "pack_corner",
        [shape((rows_e, LANES), BF)] * 2 + [shape((rows_y, LANES), BF)] * 2,
        scalars=2,
    )(side, odd_y, inner_y, outer_y)
    corner = inner
    inner, outer = exchange(inner, outer, "gx")
    w1, w2, w3 = local_call(
        weights_body,
        "weights",
        [
            shape((4 * taps // 3 * w_first.shape[1], 2 * chan), BF),
            shape((4 * taps // 3 * chan, 2 * chan), BF),
            shape((4 * taps // 3 * chan, 2 * chan), BF),
        ],
        [
            pltpu.VMEM(w_first.shape, BF),
            pltpu.VMEM(w_second.shape, BF),
            pltpu.SemaphoreType.DMA((2,)),
        ],
        in_hbm=(0, 1),
    )(w_first, w_second, corner)
    rows = chan // 2 + w_first.shape[1] // 2
    pairs = (kz, 2 * chan)
    features, sent, kept = local_call(
        part(compute_body, cx, cy, kz),
        "compute",
        [
            shape((cx, cy, 2 * kz, chan), BF),
            shape((taps, rows, chan), BF),
            shape((taps, rows, chan), F32),
        ],
        [pltpu.VMEM((rows_x, LANES), BF)] * 2
        + [pltpu.VMEM((rows_e, LANES), BF)] * 2
        + [
            pltpu.VMEM((ex, ey, kz, LANES), BF),
            pltpu.VMEM((ex, ey, kz, LANES), BF),
            pltpu.VMEM((cx + 4, cy + 4, *pairs), BF),
            pltpu.VMEM((cx + 4, cy + 4, *pairs), BF),
            pltpu.VMEM((cx + 4, cy + 4, *pairs), BF),
            pltpu.VMEM(((cx + 2) * uy * 2 * kz, LANES), F32),
            pltpu.VMEM(((cx + 2) * uy * 2 * kz, LANES), F32),
            pltpu.VMEM((cx + 2, uy, *pairs), BF),
            pltpu.VMEM((cx + 2, uy, *pairs), BF),
            pltpu.VMEM((cx, cy, *pairs), F32),
            pltpu.VMEM((cx * cy * kz, 2 * chan), BF),
            pltpu.VMEM(w_second.shape, F32),
            pltpu.VMEM(w_first.shape, F32),
            pltpu.VMEM((cx, cy, 2 * kz, chan), BF),
            pltpu.SemaphoreType.DMA(()),
        ],
        scalars=1,
        out_hbm=(0,),
        limit=32,
    )(side, field, up, tile, left, right, inner_x, outer_x, inner, outer, w1, b_first.reshape(1, -1), w2, b_second.reshape(1, -1), w3)
    sent, kept = sent.reshape(-1, chan), kept.reshape(-1, chan)
    cut = kept.shape[0] // 2
    total = [
        kept_half + swap(sent_half, core).astype(F32)
        for sent_half, kept_half in ((sent[:cut], kept[:cut]), (sent[cut:], kept[cut:]))
    ]
    own = summed_everywhere(total, levels[1:])
    other = [swap(part_of, core) for part_of in own]
    step_second, step_first = local_call(
        norm_body,
        "normalize",
        [shape(w_second.shape, F32), shape(w_first.shape, F32)],
        [
            pltpu.VMEM(w_second.shape, F32),
            pltpu.VMEM(w_first.shape, F32),
            pltpu.SemaphoreType.DMA((18,)),
        ],
        scalars=1,
        out_hbm=(0, 1),
    )(side, *own, *other)
    return (features, step_first, step_second)


def solution(mesh):
    in_specs = (
        P("gx", "gy", None, None),
        P("gx", "gy", None),
        P(),
        P(),
        P(),
        P(),
        P("gx", "gy", None, None),
    )
    out_specs = (P("gx", "gy", None, None), P(), P())
    return jax.shard_map(
        on_device, mesh=mesh, in_specs=in_specs, out_specs=out_specs, check_vma=False
    )
```

```python
import functools

import jax
import jax.numpy as jnp
from jax import lax
from jax.experimental import pallas as pl
from jax.experimental.pallas import tpu as pltpu
from jax.sharding import PartitionSpec as P

BF = jnp.bfloat16
F32 = jnp.float32
LANES = 128
FIELD_HALO = 3
CHAINS = 3
MASK_HALO = 2


def bit_levels(axes):
    levels = []
    for axis in axes:
        bit = 1
        while bit < lax.axis_size(axis):
            levels.append((axis, bit))
            bit *= 2
    return levels


def swap(part, level):
    axis, bit = level
    return lax.ppermute(part, axis, [(i, i ^ bit) for i in range(lax.axis_size(axis))])


def side_of(level):
    axis, bit = level
    return lax.rem(lax.axis_index(axis) // bit, 2)


def halves(part, level):
    half = part.shape[0] // 2
    side = side_of(level)
    sent = lax.dynamic_slice_in_dim(part, (1 - side) * half, half, 0).astype(BF)
    kept = lax.dynamic_slice_in_dim(part, side * half, half, 0)
    return sent, kept


def joined(own, other, level):
    return jnp.where(
        side_of(level) == 0,
        jnp.concatenate([own, other], axis=0),
        jnp.concatenate([other, own], axis=0),
    )


def summed_everywhere(total, levels):
    early, final = levels[:-1], levels[-1]
    pieces = 2 ** len(early)
    rows = [part.shape[0] for part in total]
    parts = [jnp.pad(part, ((0, -part.shape[0] % pieces), (0, 0))) for part in total]
    turns = [i % len(early) for i in range(len(parts))]
    steps = list(zip(*(early[i:] + early[:i] for i in turns)))
    for order in steps:
        split = [halves(part, level) for part, level in zip(parts, order)]
        got = [swap(sent, level) for (sent, _), level in zip(split, order)]
        parts = [kept + other.astype(F32) for (_, kept), other in zip(split, got)]
    parts = [part.astype(BF) for part in parts]
    parts = [(part.astype(F32) + swap(part, final).astype(F32)).astype(BF) for part in parts]
    for order in reversed(steps):
        got = [swap(part, level) for part, level in zip(parts, order)]
        parts = [joined(own, other, level) for own, other, level in zip(parts, got, order)]
    return [part[:count] for part, count in zip(parts, rows)]


def exchange(inner, outer, axis):
    count = lax.axis_size(axis)
    pairs = [(i, i + 1) for i in range(1, count - 1, 2)]
    outer = lax.ppermute(outer, axis, pairs + [(b, a) for a, b in pairs])
    inner = lax.ppermute(inner, axis, [(i, i ^ 1) for i in range(count)])
    return inner, outer


def ends_of(odd, inner, outer):
    first, second = inner[...], outer[...]
    return jnp.where(odd, first, second), jnp.where(odd, second, first)


def put_rows(ref, parts):
    row = 0
    for part in parts:
        rows = part.reshape(-1, LANES)
        ref[row : row + rows.shape[0]] = rows
        row += rows.shape[0]


def pack_own_body(
    cx, cy, kz, odd, odd_y, hfield, hup, hmask,
    inner_y, outer_y, inner_x, outer_x, tile, field, up,
    mask, square, deep, sems,
):
    fh = FIELD_HALO
    pairs = (
        (hmask, mask),
        (hfield, field),
        (hup, up),
    )
    copies = [
        pltpu.make_async_copy(source, target, sems.at[i])
        for i, (source, target) in enumerate(pairs)
    ]
    for copy in copies:
        copy.start()
    cells = cx * cy
    square[...] = jnp.zeros_like(square)
    copies[0].wait()
    square[0:cells, 0 : 2 * kz] = mask[...].reshape(cells, 2 * kz).astype(F32)
    deep[...] = square[...].T
    at_even = deep[pl.ds(0, kz, stride=2), :]
    at_odd = deep[pl.ds(1, kz, stride=2), :]
    tile[...] = (at_even + pltpu.roll(at_odd, LANES // 2, 1)).astype(BF)
    copies[1].wait()
    copies[2].wait()
    for ref, end in ((inner_y, 1 - odd_y[0]), (outer_y, odd_y[0])):
        put_rows(
            ref,
            (field[:, pl.ds(end * (cy - fh), fh)], up[:, pl.ds(end * (cy - 1), 1)], tile[...]),
        )
    for ref, end in ((inner_x, 1 - odd[0]), (outer_x, odd[0])):
        put_rows(
            ref, (field[pl.ds(end * (cx - fh), fh)], up[pl.ds(end * (cx - 1), 1)], tile[...])
        )


def pack_corner_body(cx, cy, kz, odd, odd_y, inner_y, outer_y, inner, outer, left, right):
    left[...], right[...] = ends_of(odd_y[0] == 1, inner_y, outer_y)
    fh = FIELD_HALO
    nf, nu = cx * fh * kz, cx * 2 * kz
    for ref, end in ((inner, 1 - odd[0]), (outer, odd[0])):
        parts = []
        for r in range(fh):
            at = pl.multiple_of((end * (cx - fh) + r) * fh * kz, kz)
            parts += [left[pl.ds(at, fh * kz)], right[pl.ds(at, fh * kz)]]
        at = pl.multiple_of(nf + end * (cx - 1) * 2 * kz, kz)
        parts += [left[pl.ds(at, 2 * kz)], right[pl.ds(at, 2 * kz)]]
        parts += [left[nf + nu :], right[nf + nu :]]
        put_rows(ref, parts)


def side_pair(pair, kz, width):
    rows = pair.shape[0]
    depth = lax.rem(lax.broadcasted_iota(jnp.int32, (rows, width), 0), kz)
    above = pltpu.roll(pair[:, :width], rows - 1, 0)
    below = pltpu.roll(pair[:, width:], 1, 0)
    above = jnp.where(depth == kz - 1, 0.0, above)
    below = jnp.where(depth == 0, 0.0, below)
    return above, below


def taps_of(pair, side, at, rows, cols):
    parts = []
    for a in range(3):
        for b in range(3):
            for ref in (pair, side):
                part = ref[pl.ds(at + a, rows), b : b + cols]
                parts.append(part.reshape(-1, part.shape[-1]))
    return jnp.concatenate(parts, axis=1)


def compute_body(
    cx, cy, kz,
    side, field, up, tile, left, right, inner_x, outer_x, inner, outer, w1, b1, w2, b2, second_taps,
    features, sent, kept,
    low, high, low_ends, high_ends,
    xp, xs, hp, hs, act, upf, outf, g2p, g2s, gate, g1, d2, d1, shown, w3, sem,
):
    low[...], high[...] = ends_of(side[0] == 1, inner_x, outer_x)
    low_ends[...], high_ends[...] = ends_of(side[0] == 1, inner, outer)
    fh, mh = FIELD_HALO, MASK_HALO
    ex, ey, uy = cx + 2 * fh, cy + 2 * fh, cy + 2
    nf, nu = cx * fh * kz, cx * 2 * kz
    nx, nw = fh * cy * kz, cy * 2 * kz
    ne, nv = fh * 2 * fh * kz, 2 * kz
    xp[fh : fh + cx, fh : fh + cy] = field[...]
    xp[fh : fh + cx, 0:fh] = left[0:nf].reshape(cx, fh, kz, LANES)
    xp[fh : fh + cx, fh + cy :] = right[0:nf].reshape(cx, fh, kz, LANES)
    for at, own, ends in ((0, low, low_ends), (fh + cx, high, high_ends)):
        xp[at : at + fh, fh : fh + cy] = own[0:nx].reshape(fh, cy, kz, LANES)
        block = ends[0:ne].reshape(fh, 2 * fh, kz, LANES)
        xp[at : at + fh, 0:fh] = block[:, :fh]
        xp[at : at + fh, fh + cy :] = block[:, fh:]

    def fill_side(i):
        rows = xp[i].reshape(ey * kz, LANES).astype(F32)
        depth = lax.rem(lax.broadcasted_iota(jnp.int32, rows.shape, 0), kz)
        lane = lax.broadcasted_iota(jnp.int32, rows.shape, 1)
        above = jnp.where(depth == kz - 1, 0.0, pltpu.roll(rows, ey * kz - 1, 0))
        below = jnp.where(depth == 0, 0.0, pltpu.roll(rows, 1, 0))
        both = jnp.where(lane < LANES // 2, above, below).astype(BF)
        xs[i] = both.reshape(ey, kz, LANES)
    for i in range(ex):
        fill_side(i)
    span = uy * 2 * kz

    def put_up(x, y, cols, value):
        base = x * span + y * 2 * kz
        upf[base : base + cols * 2 * kz] = value.reshape(-1, LANES).astype(F32)

    for x, own, ends in ((0, low, low_ends), (cx + 1, high, high_ends)):
        put_up(x, 1, cy, own[nx : nx + nw])
        put_up(x, 0, 1, ends[ne : ne + nv])
        put_up(x, cy + 1, 1, ends[ne + nv : ne + 2 * nv])
    for x in range(cx):
        at = nf + x * 2 * kz
        put_up(x + 1, 0, 1, left[at : at + 2 * kz])
        put_up(x + 1, 1, cy, up[x])
        put_up(x + 1, cy + 1, 1, right[at : at + 2 * kz])

    def put_mask(source, sx, sy, x, y):
        for parity in range(2):
            lane = sx * cy + sy + parity * (LANES // 2)
            value = jnp.broadcast_to(source[:, lane : lane + 1], (kz, LANES))
            act[x, y, :, parity * LANES : (parity + 1) * LANES] = value.astype(BF)

    def three(ends, own):
        at = ne + 2 * nv
        rows = ends[at : at + kz], own[nx + nw :], ends[at + kz :]
        return [part.astype(F32) for part in rows]

    rows_mid = [left[nf + nu :].astype(F32), tile[...].astype(F32), right[nf + nu :].astype(F32)]
    rows_low, rows_high = three(low_ends, low), three(high_ends, high)
    for x in range(cx + 2 * mh):
        if x < mh:
            sources, sx = rows_low, cx - mh + x
        elif x < mh + cx:
            sources, sx = rows_mid, x - mh
        else:
            sources, sx = rows_high, x - mh - cx
        for y in range(cy):
            put_mask(sources[1], sx, y, x, mh + y)
        for j in range(mh):
            put_mask(sources[0], sx, cy - mh + j, x, j)
            put_mask(sources[2], sx, j, x, mh + cy + j)

    bias1 = jnp.concatenate([b1[...], b1[...]], axis=1)
    bias2 = jnp.concatenate([b2[...], b2[...]], axis=1)

    hx, hy = cx + 4, cy + 4
    step = 1

    def first(i):
        at = i * step
        window = taps_of(xp, xs, at, step, hy)
        z = jnp.dot(window, w1[...], preferred_element_type=F32) + bias1
        s = jax.nn.sigmoid(z)
        m = act[pl.ds(at, step)].reshape(step * hy * kz, 2 * LANES).astype(F32)
        h = z * s * m
        above, below = side_pair(h, kz, LANES)
        hp[pl.ds(at, step)] = h.astype(BF).reshape(step, hy, kz, 2 * LANES)
        both = jnp.concatenate([above, below], axis=1).astype(BF)
        hs[pl.ds(at, step)] = both.reshape(step, hy, kz, 2 * LANES)

        if 2 // step <= i < (2 + cx) // step:
            factor = m * s * (1.0 + z * (1.0 - s))
            factor = factor.reshape(step, hy, kz, 2 * LANES)[:, 2 : 2 + cy]
            gate[pl.ds(at - 2, step)] = factor

    for i in range(hx // step):
        first(i)

    taps, chan = second_taps.shape[:2]
    for g in range(taps // 3):
        block = [second_taps[taps - 1 - 3 * g - c].astype(F32).T.astype(BF) for c in range(3)]
        put_pair_weights(w3, g * 4 * chan, block)

    def second(i):
        at = i * step
        window = taps_of(hp, hs, at, step, uy)
        z = jnp.dot(window, w2[...], preferred_element_type=F32) + bias2
        s = jax.nn.sigmoid(z)
        m = act[pl.ds(at + 1, step), 1 : 1 + uy].reshape(-1, 2 * LANES).astype(F32)
        rows = step * uy * kz
        base = at * span
        u = jnp.concatenate(
            [upf[pl.ds(base, rows, stride=2), :], upf[pl.ds(base + 1, rows, stride=2), :]], axis=1
        )
        g = u * m * s * (1.0 + z * (1.0 - s))
        gb = g.astype(BF)
        above, below = side_pair(g, kz, LANES)
        g2p[pl.ds(at, step)] = gb.reshape(step, uy, kz, 2 * LANES)
        both = jnp.concatenate([above, below], axis=1).astype(BF)
        g2s[pl.ds(at, step)] = both.reshape(step, uy, kz, 2 * LANES)
        out = z * s * m
        outf[pl.ds(base, rows, stride=2), :] = out[:, :LANES]
        outf[pl.ds(base + 1, rows, stride=2), :] = out[:, LANES:]
    for i in range((cx + 2) // step):
        second(i)
    for x in range(cx):
        base = (x + 1) * span + 2 * kz
        rows = outf[base : base + cy * 2 * kz].astype(BF)
        shown[x] = rows.reshape(cy, 2 * kz, LANES)
    show = pltpu.make_async_copy(shown, features, sem)
    show.start()

    own = hp[2 : 2 + cx, 2 : 2 + cy].reshape(-1, 2 * LANES)
    turned = own.T
    for a in range(3):
        for b in range(3):
            parts = [
                ref[2 - a : 2 - a + cx, 2 - b : 2 - b + cy].reshape(-1, 2 * LANES)
                for ref in (g2p, g2s)
            ]
            for half, part in enumerate(parts):
                block = jnp.dot(turned, part, preferred_element_type=F32)
                q = [[block[r * LANES : (r + 1) * LANES, c * LANES : (c + 1) * LANES] for c in (0, 1)] for r in (0, 1)]
                t = 9 * a + 3 * b
                if half == 0:
                    d2[t + 1] = q[0][0] + q[1][1]
                    d2[t] = q[0][1]
                    d2[t + 2] = q[1][0]
                else:
                    d2[t] = d2[t] + q[1][0]
                    d2[t + 2] = d2[t + 2] + q[0][1]

    rows = step * cy * kz

    def grad(i):
        at = i * step
        window = taps_of(g2p, g2s, at, step, cy)
        e = jnp.dot(window, w3[...], preferred_element_type=F32)
        g = e * gate[pl.ds(at, step)].reshape(rows, 2 * LANES)
        g1[i * rows : (i + 1) * rows] = g.astype(BF)
    for i in range(cx // step):
        grad(i)
    right_side = g1[...]
    cells = cx * cy * kz
    half = LANES // 2
    for b in range(3):
        cols = slice(fh - 1 + b, fh - 1 + b + cy)
        parts = [ref[fh - 1 : fh + 1 + cx, cols].reshape(-1, LANES) for ref in (xp, xs)]
        turned = jnp.concatenate(parts, axis=1).T
        for a in range(3):
            at = a * cy * kz
            block = jnp.dot(turned[:, at : at + cells], right_side, preferred_element_type=F32)
            q = [
                [block[r * half : (r + 1) * half, c * LANES : (c + 1) * LANES] for c in (0, 1)]
                for r in range(4)
            ]
            t = 9 * a + 3 * b
            d1[t] = q[0][1] + q[3][0]
            d1[t + 1] = q[0][0] + q[1][1]
            d1[t + 2] = q[1][0] + q[2][1]
    at = 0
    for total in (d2, d1):
        half = total.shape[1] // 2
        mine = pl.multiple_of(side[0] * half, half)
        other = pl.multiple_of((1 - side[0]) * half, half)
        sent[:, at : at + half] = total[:, pl.ds(other, half)].astype(BF)
        kept[:, at : at + half] = total[:, pl.ds(mine, half)]
        at += half
    show.wait()


def norm_body(chains, side, *refs):
    own, other = refs[:chains], refs[chains : 2 * chains]
    out2, out1, held2, held1, sems = refs[2 * chains :]
    taps = out2.shape[0]
    rows_of = held2.shape[1] // 2, held1.shape[1] // 2
    stride = sum(rows_of)

    def rows(refs, start, count):
        parts = []
        for ref in refs:
            low, high = max(start, 0), min(start + count, ref.shape[0])
            if low < high:
                parts.append(ref[low:high])
            start -= ref.shape[0]
        return jnp.concatenate(parts, axis=0).astype(F32)

    def spans():
        for t in range(taps):
            for i, at in ((0, t * stride), (1, t * stride + rows_of[0])):
                yield t, i, at

    squares = [jnp.zeros((8, LANES), F32), jnp.zeros((8, LANES), F32)]
    for t, i, at in spans():
        for pair in (own, other):
            value = rows(pair, at, rows_of[i])
            squares[i] += jnp.sum((value * value).reshape(-1, 8, LANES), axis=0)
    scales = [
        lax.rsqrt(jnp.full((1, LANES), jnp.sum(total)) / float(out.size) + 1e-06)
        for total, out in zip(squares, (out2, out1))
    ]
    group = taps // 3
    copies = []
    for t, i, at in spans():
        held, count = (held2, held1)[i], rows_of[i]
        mine = pl.multiple_of(side[0] * count, count)
        rest = pl.multiple_of((1 - side[0]) * count, count)
        held[t, pl.ds(mine, count)] = rows(own, at, count) * scales[i]
        held[t, pl.ds(rest, count)] = rows(other, at, count) * scales[i]
        if i == 1 and (t + 1) % group == 0:
            span = pl.ds(t + 1 - group, group)
            for held, out in ((held2, out2), (held1, out1)):
                copy = pltpu.make_async_copy(held.at[span], out.at[span], sems.at[len(copies)])
                copy.start()
                copies.append(copy)
    for copy in copies:
        copy.wait()


PAIR_TAPS = ((1, 0), (2, 1), (None, 2), (0, None))


def put_pair_weights(out, at, block):
    depth, width = block[0].shape
    none = jnp.zeros((depth, width), BF)
    for r, row in enumerate(PAIR_TAPS):
        for c, tap in enumerate(row):
            value = none if tap is None else block[tap]
            out[pl.ds(at + r * depth, depth), c * width : (c + 1) * width] = value


def weights_body(hfirst, hsecond, _, w1, w2, second, first, sems):
    copies = [
        pltpu.make_async_copy(hfirst, first, sems.at[0]),
        pltpu.make_async_copy(hsecond, second, sems.at[1]),
    ]
    for copy in copies:
        copy.start()
    for copy, source, out in zip(copies, (first, second), (w1, w2)):
        copy.wait()
        depth = source.shape[1]

        @pl.loop(0, source.shape[0] // 3)
        def _(g):
            block = [source[3 * g + c] for c in range(3)]
            put_pair_weights(out, pl.multiple_of(g * 4 * depth, depth), block)


def local_call(body, name, out, scratch=(), scalars=0, in_hbm=(), out_hbm=(), limit=24):
    def call(*args):
        vmem = pl.BlockSpec(memory_space=pltpu.VMEM)
        hbm = pl.BlockSpec(memory_space=pltpu.HBM)
        ins = [
            pl.BlockSpec(memory_space=pltpu.SMEM) if i < scalars else hbm if i in in_hbm else vmem
            for i in range(len(args))
        ]
        held = [
            a
            if i < scalars
            else pltpu.with_memory_space_constraint(a, pltpu.HBM if i in in_hbm else pltpu.VMEM)
            for i, a in enumerate(args)
        ]
        outs = [
            (pltpu.HBM if i in out_hbm else pltpu.VMEM)(o.shape, o.dtype) for i, o in enumerate(out)
        ]
        return pl.pallas_call(
            body,
            out_shape=outs,
            in_specs=ins,
            out_specs=[hbm if i in out_hbm else vmem for i in range(len(out))],
            scratch_shapes=list(scratch),
            compiler_params=pltpu.CompilerParams(vmem_limit_bytes=limit << 20),
            name=name,
        )(*held)

    return call


def on_device(volume, basin_mask, w_first, b_first, w_second, b_second, upstream):
    cx, cy, kz, _ = volume.shape
    taps, _, chan = w_first.shape
    part = functools.partial
    shape = jax.ShapeDtypeStruct
    levels = bit_levels(("gx", "gy"))
    core = levels[0]
    side = side_of(core).astype(jnp.int32).reshape(1)
    odd_y = side_of(("gy", 1)).astype(jnp.int32).reshape(1)
    ex, ey, uy = cx + 2 * FIELD_HALO, cy + 2 * FIELD_HALO, cy + 2
    rows_y = cx * FIELD_HALO * kz + cx * 2 * kz + kz
    rows_x = FIELD_HALO * cy * kz + cy * 2 * kz + kz
    rows_e = FIELD_HALO * 2 * FIELD_HALO * kz + 2 * 2 * kz + 2 * kz
    inner_y, outer_y, inner_x, outer_x, tile, field, up = local_call(
        part(pack_own_body, cx, cy, kz),
        "pack_own",
        [shape((rows_y, LANES), BF)] * 2
        + [shape((rows_x, LANES), BF)] * 2
        + [shape((kz, LANES), BF)]
        + [shape(a.shape, BF) for a in (volume, upstream)],
        [pltpu.VMEM(basin_mask.shape, jnp.int32)]
        + [pltpu.VMEM((LANES, LANES), F32)] * 2
        + [pltpu.SemaphoreType.DMA((3,))],
        scalars=2,
        in_hbm=(2, 3, 4),
    )(side, odd_y, volume, upstream, basin_mask)
    inner_y, outer_y = exchange(inner_y, outer_y, "gy")
    inner_x, outer_x = exchange(inner_x, outer_x, "gx")
    inner, outer, left, right = local_call(
        part(pack_corner_body, cx, cy, kz),
        "pack_corner",
        [shape((rows_e, LANES), BF)] * 2 + [shape((rows_y, LANES), BF)] * 2,
        scalars=2,
    )(side, odd_y, inner_y, outer_y)
    corner = inner
    inner, outer = exchange(inner, outer, "gx")
    w1, w2, second_taps = local_call(
        weights_body,
        "weights",
        [
            shape((4 * taps // 3 * w_first.shape[1], 2 * chan), BF),
            shape((4 * taps // 3 * chan, 2 * chan), BF),
            shape(w_second.shape, BF),
        ],
        [pltpu.VMEM(w_first.shape, BF), pltpu.SemaphoreType.DMA((2,))],
        in_hbm=(0, 1),
    )(w_first, w_second, corner)
    rows = chan // 2 + w_first.shape[1] // 2
    pairs = (kz, 2 * chan)
    features, sent, kept = local_call(
        part(compute_body, cx, cy, kz),
        "compute",
        [
            shape((cx, cy, 2 * kz, chan), BF),
            shape((taps, rows, chan), BF),
            shape((taps, rows, chan), F32),
        ],
        [pltpu.VMEM((rows_x, LANES), BF)] * 2
        + [pltpu.VMEM((rows_e, LANES), BF)] * 2
        + [
            pltpu.VMEM((ex, ey, kz, LANES), BF),
            pltpu.VMEM((ex, ey, kz, LANES), BF),
            pltpu.VMEM((cx + 4, cy + 4, *pairs), BF),
            pltpu.VMEM((cx + 4, cy + 4, *pairs), BF),
            pltpu.VMEM((cx + 4, cy + 4, *pairs), BF),
            pltpu.VMEM(((cx + 2) * uy * 2 * kz, LANES), F32),
            pltpu.VMEM(((cx + 2) * uy * 2 * kz, LANES), F32),
            pltpu.VMEM((cx + 2, uy, *pairs), BF),
            pltpu.VMEM((cx + 2, uy, *pairs), BF),
            pltpu.VMEM((cx, cy, *pairs), F32),
            pltpu.VMEM((cx * cy * kz, 2 * chan), BF),
            pltpu.VMEM(w_second.shape, F32),
            pltpu.VMEM(w_first.shape, F32),
            pltpu.VMEM((cx, cy, 2 * kz, chan), BF),
            pltpu.VMEM((4 * taps // 3 * chan, 2 * chan), BF),
            pltpu.SemaphoreType.DMA(()),
        ],
        scalars=1,
        out_hbm=(0,),
        limit=32,
    )(side, field, up, tile, left, right, inner_x, outer_x, inner, outer, w1, b_first.reshape(1, -1), w2, b_second.reshape(1, -1), second_taps)
    sent, kept = sent.reshape(-1, chan), kept.reshape(-1, chan)
    cut = kept.shape[0] // CHAINS
    total = []
    for i in range(CHAINS):
        span = slice(i * cut, (i + 1) * cut)
        total.append(kept[span] + swap(sent[span], core).astype(F32))
    own = summed_everywhere(total, levels[1:])
    other = [swap(part_of, core) for part_of in own]
    step_second, step_first = local_call(
        part(norm_body, CHAINS),
        "normalize",
        [shape(w_second.shape, F32), shape(w_first.shape, F32)],
        [
            pltpu.VMEM(w_second.shape, F32),
            pltpu.VMEM(w_first.shape, F32),
            pltpu.SemaphoreType.DMA((6,)),
        ],
        scalars=1,
        out_hbm=(0, 1),
    )(side, *own, *other)
    return (features, step_first, step_second)


def solution(mesh):
    in_specs = (
        P("gx", "gy", None, None),
        P("gx", "gy", None),
        P(),
        P(),
        P(),
        P(),
        P("gx", "gy", None, None),
    )
    out_specs = (P("gx", "gy", None, None), P(), P())
    return jax.shard_map(
        on_device, mesh=mesh, in_specs=in_specs, out_specs=out_specs, check_vma=False
    )
```

```python
import functools

import jax
import jax.numpy as jnp
from jax import lax
from jax.experimental import pallas as pl
from jax.experimental.pallas import tpu as pltpu
from jax.sharding import PartitionSpec as P

BF = jnp.bfloat16
F32 = jnp.float32
LANES = 128
FIELD_HALO = 3
CHAINS = 3
MASK_HALO = 2


def bit_levels(axes):
    levels = []
    for axis in axes:
        bit = 1
        while bit < lax.axis_size(axis):
            levels.append((axis, bit))
            bit *= 2
    return levels


def swap(part, level):
    axis, bit = level
    return lax.ppermute(part, axis, [(i, i ^ bit) for i in range(lax.axis_size(axis))])


def side_of(level):
    axis, bit = level
    return lax.rem(lax.axis_index(axis) // bit, 2)


def halves(part, level):
    half = part.shape[0] // 2
    side = side_of(level)
    sent = lax.dynamic_slice_in_dim(part, (1 - side) * half, half, 0).astype(BF)
    kept = lax.dynamic_slice_in_dim(part, side * half, half, 0)
    return sent, kept


def joined(own, other, level):
    return jnp.where(
        side_of(level) == 0,
        jnp.concatenate([own, other], axis=0),
        jnp.concatenate([other, own], axis=0),
    )


def summed_everywhere(total, levels):
    early, final = levels[:-1], levels[-1]
    pieces = 2 ** len(early)
    rows = [part.shape[0] for part in total]
    parts = [jnp.pad(part, ((0, -part.shape[0] % pieces), (0, 0))) for part in total]
    turns = [i % len(early) for i in range(len(parts))]
    steps = list(zip(*(early[i:] + early[:i] for i in turns)))
    for order in steps:
        split = [halves(part, level) for part, level in zip(parts, order)]
        got = [swap(sent, level) for (sent, _), level in zip(split, order)]
        parts = [kept + other.astype(F32) for (_, kept), other in zip(split, got)]
    parts = [part.astype(BF) for part in parts]
    parts = [(part.astype(F32) + swap(part, final).astype(F32)).astype(BF) for part in parts]
    for order in reversed(steps):
        got = [swap(part, level) for part, level in zip(parts, order)]
        parts = [joined(own, other, level) for own, other, level in zip(parts, got, order)]
    return [part[:count] for part, count in zip(parts, rows)]


def exchange(inner, outer, axis):
    count = lax.axis_size(axis)
    pairs = [(i, i + 1) for i in range(1, count - 1, 2)]
    outer = lax.ppermute(outer, axis, pairs + [(b, a) for a, b in pairs])
    inner = lax.ppermute(inner, axis, [(i, i ^ 1) for i in range(count)])
    return inner, outer


def ends_of(odd, inner, outer):
    first, second = inner[...], outer[...]
    return jnp.where(odd, first, second), jnp.where(odd, second, first)


def put_rows(ref, parts):
    row = 0
    for part in parts:
        rows = part.reshape(-1, LANES)
        ref[row : row + rows.shape[0]] = rows
        row += rows.shape[0]


def pack_own_body(
    cx, cy, kz, odd, odd_y, hfield, hup, hmask,
    inner_y, outer_y, inner_x, outer_x, tile, field, up,
    mask, square, deep, sems,
):
    fh = FIELD_HALO
    pairs = (
        (hmask, mask),
        (hfield, field),
        (hup, up),
    )
    copies = [
        pltpu.make_async_copy(source, target, sems.at[i])
        for i, (source, target) in enumerate(pairs)
    ]
    for copy in copies:
        copy.start()
    cells = cx * cy
    square[...] = jnp.zeros_like(square)
    copies[0].wait()
    square[0:cells, 0 : 2 * kz] = mask[...].reshape(cells, 2 * kz).astype(F32)
    deep[...] = square[...].T
    at_even = deep[pl.ds(0, kz, stride=2), :]
    at_odd = deep[pl.ds(1, kz, stride=2), :]
    tile[...] = (at_even + pltpu.roll(at_odd, LANES // 2, 1)).astype(BF)
    copies[1].wait()
    copies[2].wait()
    for ref, end in ((inner_y, 1 - odd_y[0]), (outer_y, odd_y[0])):
        put_rows(
            ref,
            (field[:, pl.ds(end * (cy - fh), fh)], up[:, pl.ds(end * (cy - 1), 1)], tile[...]),
        )
    for ref, end in ((inner_x, 1 - odd[0]), (outer_x, odd[0])):
        put_rows(
            ref, (field[pl.ds(end * (cx - fh), fh)], up[pl.ds(end * (cx - 1), 1)], tile[...])
        )


def pack_corner_body(cx, cy, kz, odd, odd_y, inner_y, outer_y, inner, outer, left, right):
    left[...], right[...] = ends_of(odd_y[0] == 1, inner_y, outer_y)
    fh = FIELD_HALO
    nf, nu = cx * fh * kz, cx * 2 * kz
    for ref, end in ((inner, 1 - odd[0]), (outer, odd[0])):
        parts = []
        for r in range(fh):
            at = pl.multiple_of((end * (cx - fh) + r) * fh * kz, kz)
            parts += [left[pl.ds(at, fh * kz)], right[pl.ds(at, fh * kz)]]
        at = pl.multiple_of(nf + end * (cx - 1) * 2 * kz, kz)
        parts += [left[pl.ds(at, 2 * kz)], right[pl.ds(at, 2 * kz)]]
        parts += [left[nf + nu :], right[nf + nu :]]
        put_rows(ref, parts)


def side_pair(pair, kz, width):
    rows = pair.shape[0]
    depth = lax.rem(lax.broadcasted_iota(jnp.int32, (rows, width), 0), kz)
    above = pltpu.roll(pair[:, :width], rows - 1, 0)
    below = pltpu.roll(pair[:, width:], 1, 0)
    above = jnp.where(depth == kz - 1, 0.0, above)
    below = jnp.where(depth == 0, 0.0, below)
    return above, below


def taps_of(pair, side, at, rows, cols):
    parts = []
    for a in range(3):
        for b in range(3):
            for ref in (pair, side):
                part = ref[pl.ds(at + a, rows), b : b + cols]
                parts.append(part.reshape(-1, part.shape[-1]))
    return jnp.concatenate(parts, axis=1)


def compute_body(
    cx, cy, kz,
    side, field, up, tile, left, right, inner_x, outer_x, inner, outer, w1, b1, w2, b2, second_taps,
    features, sent, kept,
    low, high, low_ends, high_ends,
    xp, xs, hp, hs, act, upf, outf, g2p, g2s, gate, g1, d2, d1, shown, w3, sem,
):
    low[...], high[...] = ends_of(side[0] == 1, inner_x, outer_x)
    low_ends[...], high_ends[...] = ends_of(side[0] == 1, inner, outer)
    fh, mh = FIELD_HALO, MASK_HALO
    ex, ey, uy = cx + 2 * fh, cy + 2 * fh, cy + 2
    nf, nu = cx * fh * kz, cx * 2 * kz
    nx, nw = fh * cy * kz, cy * 2 * kz
    ne, nv = fh * 2 * fh * kz, 2 * kz
    xp[fh : fh + cx, fh : fh + cy] = field[...]
    xp[fh : fh + cx, 0:fh] = left[0:nf].reshape(cx, fh, kz, LANES)
    xp[fh : fh + cx, fh + cy :] = right[0:nf].reshape(cx, fh, kz, LANES)
    for at, own, ends in ((0, low, low_ends), (fh + cx, high, high_ends)):
        xp[at : at + fh, fh : fh + cy] = own[0:nx].reshape(fh, cy, kz, LANES)
        block = ends[0:ne].reshape(fh, 2 * fh, kz, LANES)
        xp[at : at + fh, 0:fh] = block[:, :fh]
        xp[at : at + fh, fh + cy :] = block[:, fh:]

    def fill_side(i):
        rows = xp[i].reshape(ey * kz, LANES).astype(F32)
        depth = lax.rem(lax.broadcasted_iota(jnp.int32, rows.shape, 0), kz)
        lane = lax.broadcasted_iota(jnp.int32, rows.shape, 1)
        above = jnp.where(depth == kz - 1, 0.0, pltpu.roll(rows, ey * kz - 1, 0))
        below = jnp.where(depth == 0, 0.0, pltpu.roll(rows, 1, 0))
        both = jnp.where(lane < LANES // 2, above, below).astype(BF)
        xs[i] = both.reshape(ey, kz, LANES)
    for i in range(ex):
        fill_side(i)
    span = uy * 2 * kz

    def put_up(x, y, cols, value):
        base = x * span + y * 2 * kz
        upf[base : base + cols * 2 * kz] = value.reshape(-1, LANES).astype(F32)

    for x, own, ends in ((0, low, low_ends), (cx + 1, high, high_ends)):
        put_up(x, 1, cy, own[nx : nx + nw])
        put_up(x, 0, 1, ends[ne : ne + nv])
        put_up(x, cy + 1, 1, ends[ne + nv : ne + 2 * nv])
    for x in range(cx):
        at = nf + x * 2 * kz
        put_up(x + 1, 0, 1, left[at : at + 2 * kz])
        put_up(x + 1, 1, cy, up[x])
        put_up(x + 1, cy + 1, 1, right[at : at + 2 * kz])

    def put_mask(source, sx, sy, x, y):
        for parity in range(2):
            lane = sx * cy + sy + parity * (LANES // 2)
            value = jnp.broadcast_to(source[:, lane : lane + 1], (kz, LANES))
            act[x, y, :, parity * LANES : (parity + 1) * LANES] = value.astype(BF)

    def three(ends, own):
        at = ne + 2 * nv
        rows = ends[at : at + kz], own[nx + nw :], ends[at + kz :]
        return [part.astype(F32) for part in rows]

    rows_mid = [left[nf + nu :].astype(F32), tile[...].astype(F32), right[nf + nu :].astype(F32)]
    rows_low, rows_high = three(low_ends, low), three(high_ends, high)
    for x in range(cx + 2 * mh):
        if x < mh:
            sources, sx = rows_low, cx - mh + x
        elif x < mh + cx:
            sources, sx = rows_mid, x - mh
        else:
            sources, sx = rows_high, x - mh - cx
        for y in range(cy):
            put_mask(sources[1], sx, y, x, mh + y)
        for j in range(mh):
            put_mask(sources[0], sx, cy - mh + j, x, j)
            put_mask(sources[2], sx, j, x, mh + cy + j)

    bias1 = jnp.concatenate([b1[...], b1[...]], axis=1)
    bias2 = jnp.concatenate([b2[...], b2[...]], axis=1)

    hx, hy = cx + 4, cy + 4
    step = 1

    def first(i):
        at = i * step
        window = taps_of(xp, xs, at, step, hy)
        z = jnp.dot(window, w1[...], preferred_element_type=F32) + bias1
        s = jax.nn.sigmoid(z)
        m = act[pl.ds(at, step)].reshape(step * hy * kz, 2 * LANES).astype(F32)
        h = z * s * m
        above, below = side_pair(h, kz, LANES)
        hp[pl.ds(at, step)] = h.astype(BF).reshape(step, hy, kz, 2 * LANES)
        both = jnp.concatenate([above, below], axis=1).astype(BF)
        hs[pl.ds(at, step)] = both.reshape(step, hy, kz, 2 * LANES)

        if 2 // step <= i < (2 + cx) // step:
            factor = m * s * (1.0 + z * (1.0 - s))
            factor = factor.reshape(step, hy, kz, 2 * LANES)[:, 2 : 2 + cy]
            gate[pl.ds(at - 2, step)] = factor

    for i in range(hx // step):
        first(i)

    taps, chan = second_taps.shape[:2]
    for g in range(taps // 3):
        block = [second_taps[taps - 1 - 3 * g - c].astype(F32).T.astype(BF) for c in range(3)]
        put_pair_weights(w3, g * 4 * chan, block)

    def second(i):
        at = i * step
        window = taps_of(hp, hs, at, step, uy)
        z = jnp.dot(window, w2[...], preferred_element_type=F32) + bias2
        s = jax.nn.sigmoid(z)
        m = act[pl.ds(at + 1, step), 1 : 1 + uy].reshape(-1, 2 * LANES).astype(F32)
        rows = step * uy * kz
        base = at * span
        u = jnp.concatenate(
            [upf[pl.ds(base, rows, stride=2), :], upf[pl.ds(base + 1, rows, stride=2), :]], axis=1
        )
        g = u * m * s * (1.0 + z * (1.0 - s))
        gb = g.astype(BF)
        above, below = side_pair(g, kz, LANES)
        g2p[pl.ds(at, step)] = gb.reshape(step, uy, kz, 2 * LANES)
        both = jnp.concatenate([above, below], axis=1).astype(BF)
        g2s[pl.ds(at, step)] = both.reshape(step, uy, kz, 2 * LANES)
        out = z * s * m
        outf[pl.ds(base, rows, stride=2), :] = out[:, :LANES]
        outf[pl.ds(base + 1, rows, stride=2), :] = out[:, LANES:]
    for i in range((cx + 2) // step):
        second(i)
    for x in range(cx):
        base = (x + 1) * span + 2 * kz
        rows = outf[base : base + cy * 2 * kz].astype(BF)
        shown[x] = rows.reshape(cy, 2 * kz, LANES)
    show = pltpu.make_async_copy(shown, features, sem)
    show.start()

    own = hp[2 : 2 + cx, 2 : 2 + cy].reshape(-1, 2 * LANES)
    turned = own.T
    for a in range(3):
        for b in range(3):
            parts = [
                ref[2 - a : 2 - a + cx, 2 - b : 2 - b + cy].reshape(-1, 2 * LANES)
                for ref in (g2p, g2s)
            ]
            for half, part in enumerate(parts):
                block = jnp.dot(turned, part, preferred_element_type=F32)
                q = [[block[r * LANES : (r + 1) * LANES, c * LANES : (c + 1) * LANES] for c in (0, 1)] for r in (0, 1)]
                t = 9 * a + 3 * b
                if half == 0:
                    d2[t + 1] = q[0][0] + q[1][1]
                    d2[t] = q[0][1]
                    d2[t + 2] = q[1][0]
                else:
                    d2[t] = d2[t] + q[1][0]
                    d2[t + 2] = d2[t + 2] + q[0][1]

    rows = step * cy * kz

    def grad(i):
        at = i * step
        window = taps_of(g2p, g2s, at, step, cy)
        e = jnp.dot(window, w3[...], preferred_element_type=F32)
        g = e * gate[pl.ds(at, step)].reshape(rows, 2 * LANES)
        g1[i * rows : (i + 1) * rows] = g.astype(BF)
    for i in range(cx // step):
        grad(i)
    right_side = g1[...]
    cells = cx * cy * kz
    half = LANES // 2
    for b in range(3):
        cols = slice(fh - 1 + b, fh - 1 + b + cy)
        parts = [ref[fh - 1 : fh + 1 + cx, cols].reshape(-1, LANES) for ref in (xp, xs)]
        turned = jnp.concatenate(parts, axis=1).T
        for a in range(3):
            at = a * cy * kz
            block = jnp.dot(turned[:, at : at + cells], right_side, preferred_element_type=F32)
            q = [
                [block[r * half : (r + 1) * half, c * LANES : (c + 1) * LANES] for c in (0, 1)]
                for r in range(4)
            ]
            t = 9 * a + 3 * b
            d1[t] = q[0][1] + q[3][0]
            d1[t + 1] = q[0][0] + q[1][1]
            d1[t + 2] = q[1][0] + q[2][1]
    at = 0
    for total in (d2, d1):
        half = total.shape[1] // 2
        mine = pl.multiple_of(side[0] * half, half)
        other = pl.multiple_of((1 - side[0]) * half, half)
        sent[:, at : at + half] = total[:, pl.ds(other, half)].astype(BF)
        kept[:, at : at + half] = total[:, pl.ds(mine, half)]
        at += half
    show.wait()


def rows_of_chains(refs, start, count):
    parts = []
    for ref in refs:
        low, high = max(start, 0), min(start + count, ref.shape[0])
        if low < high:
            parts.append(ref[low:high])
        start -= ref.shape[0]
    return jnp.concatenate(parts, axis=0).astype(F32)


def squares_of(refs, taps, rows_of):
    totals = [jnp.zeros((8, LANES), F32) for _ in rows_of]
    at = 0
    for _ in range(taps):
        for i, count in enumerate(rows_of):
            value = rows_of_chains(refs, at, count)
            totals[i] += jnp.sum((value * value).reshape(-1, 8, LANES), axis=0)
            at += count
    return totals


def squares_body(taps, rows_of, *refs):
    for i, total in enumerate(squares_of(refs[:-1], taps, rows_of)):
        refs[-1][i] = total


def norm_body(chains, side, own_squares, *refs):
    own, other = refs[:chains], refs[chains : 2 * chains]
    out2, out1, held2, held1, sems = refs[2 * chains :]
    taps = out2.shape[0]
    rows_of = held2.shape[1] // 2, held1.shape[1] // 2
    stride = sum(rows_of)

    rows = rows_of_chains

    def spans():
        for t in range(taps):
            for i, at in ((0, t * stride), (1, t * stride + rows_of[0])):
                yield t, i, at

    squares = squares_of(other, taps, rows_of)
    squares = [total + own_squares[i] for i, total in enumerate(squares)]
    scales = [
        lax.rsqrt(jnp.full((1, LANES), jnp.sum(total)) / float(out.size) + 1e-06)
        for total, out in zip(squares, (out2, out1))
    ]
    group = taps // 3
    copies = []
    for t, i, at in spans():
        held, count = (held2, held1)[i], rows_of[i]
        mine = pl.multiple_of(side[0] * count, count)
        rest = pl.multiple_of((1 - side[0]) * count, count)
        held[t, pl.ds(mine, count)] = rows(own, at, count) * scales[i]
        held[t, pl.ds(rest, count)] = rows(other, at, count) * scales[i]
        if i == 1 and (t + 1) % group == 0:
            span = pl.ds(t + 1 - group, group)
            for held, out in ((held2, out2), (held1, out1)):
                copy = pltpu.make_async_copy(held.at[span], out.at[span], sems.at[len(copies)])
                copy.start()
                copies.append(copy)
    for copy in copies:
        copy.wait()


PAIR_TAPS = ((1, 0), (2, 1), (None, 2), (0, None))


def put_pair_weights(out, at, block):
    depth, width = block[0].shape
    none = jnp.zeros((depth, width), BF)
    for r, row in enumerate(PAIR_TAPS):
        for c, tap in enumerate(row):
            value = none if tap is None else block[tap]
            out[pl.ds(at + r * depth, depth), c * width : (c + 1) * width] = value


def weights_body(hfirst, hsecond, _, w1, w2, second, first, sems):
    copies = [
        pltpu.make_async_copy(hfirst, first, sems.at[0]),
        pltpu.make_async_copy(hsecond, second, sems.at[1]),
    ]
    for copy in copies:
        copy.start()
    for copy, source, out in zip(copies, (first, second), (w1, w2)):
        copy.wait()
        depth = source.shape[1]

        @pl.loop(0, source.shape[0] // 3)
        def _(g):
            block = [source[3 * g + c] for c in range(3)]
            put_pair_weights(out, pl.multiple_of(g * 4 * depth, depth), block)


def local_call(body, name, out, scratch=(), scalars=0, in_hbm=(), out_hbm=(), limit=24):
    def call(*args):
        vmem = pl.BlockSpec(memory_space=pltpu.VMEM)
        hbm = pl.BlockSpec(memory_space=pltpu.HBM)
        ins = [
            pl.BlockSpec(memory_space=pltpu.SMEM) if i < scalars else hbm if i in in_hbm else vmem
            for i in range(len(args))
        ]
        held = [
            a
            if i < scalars
            else pltpu.with_memory_space_constraint(a, pltpu.HBM if i in in_hbm else pltpu.VMEM)
            for i, a in enumerate(args)
        ]
        outs = [
            (pltpu.HBM if i in out_hbm else pltpu.VMEM)(o.shape, o.dtype) for i, o in enumerate(out)
        ]
        return pl.pallas_call(
            body,
            out_shape=outs,
            in_specs=ins,
            out_specs=[hbm if i in out_hbm else vmem for i in range(len(out))],
            scratch_shapes=list(scratch),
            compiler_params=pltpu.CompilerParams(vmem_limit_bytes=limit << 20),
            name=name,
        )(*held)

    return call


def on_device(volume, basin_mask, w_first, b_first, w_second, b_second, upstream):
    cx, cy, kz, _ = volume.shape
    taps, _, chan = w_first.shape
    part = functools.partial
    shape = jax.ShapeDtypeStruct
    levels = bit_levels(("gx", "gy"))
    core = levels[0]
    side = side_of(core).astype(jnp.int32).reshape(1)
    odd_y = side_of(("gy", 1)).astype(jnp.int32).reshape(1)
    ex, ey, uy = cx + 2 * FIELD_HALO, cy + 2 * FIELD_HALO, cy + 2
    rows_y = cx * FIELD_HALO * kz + cx * 2 * kz + kz
    rows_x = FIELD_HALO * cy * kz + cy * 2 * kz + kz
    rows_e = FIELD_HALO * 2 * FIELD_HALO * kz + 2 * 2 * kz + 2 * kz
    inner_y, outer_y, inner_x, outer_x, tile, field, up = local_call(
        part(pack_own_body, cx, cy, kz),
        "pack_own",
        [shape((rows_y, LANES), BF)] * 2
        + [shape((rows_x, LANES), BF)] * 2
        + [shape((kz, LANES), BF)]
        + [shape(a.shape, BF) for a in (volume, upstream)],
        [pltpu.VMEM(basin_mask.shape, jnp.int32)]
        + [pltpu.VMEM((LANES, LANES), F32)] * 2
        + [pltpu.SemaphoreType.DMA((3,))],
        scalars=2,
        in_hbm=(2, 3, 4),
    )(side, odd_y, volume, upstream, basin_mask)
    inner_y, outer_y = exchange(inner_y, outer_y, "gy")
    inner_x, outer_x = exchange(inner_x, outer_x, "gx")
    inner, outer, left, right = local_call(
        part(pack_corner_body, cx, cy, kz),
        "pack_corner",
        [shape((rows_e, LANES), BF)] * 2 + [shape((rows_y, LANES), BF)] * 2,
        scalars=2,
    )(side, odd_y, inner_y, outer_y)
    corner = inner
    inner, outer = exchange(inner, outer, "gx")
    w1, w2, second_taps = local_call(
        weights_body,
        "weights",
        [
            shape((4 * taps // 3 * w_first.shape[1], 2 * chan), BF),
            shape((4 * taps // 3 * chan, 2 * chan), BF),
            shape(w_second.shape, BF),
        ],
        [pltpu.VMEM(w_first.shape, BF), pltpu.SemaphoreType.DMA((2,))],
        in_hbm=(0, 1),
    )(w_first, w_second, corner)
    rows = chan // 2 + w_first.shape[1] // 2
    pairs = (kz, 2 * chan)
    features, sent, kept = local_call(
        part(compute_body, cx, cy, kz),
        "compute",
        [
            shape((cx, cy, 2 * kz, chan), BF),
            shape((taps, rows, chan), BF),
            shape((taps, rows, chan), F32),
        ],
        [pltpu.VMEM((rows_x, LANES), BF)] * 2
        + [pltpu.VMEM((rows_e, LANES), BF)] * 2
        + [
            pltpu.VMEM((ex, ey, kz, LANES), BF),
            pltpu.VMEM((ex, ey, kz, LANES), BF),
            pltpu.VMEM((cx + 4, cy + 4, *pairs), BF),
            pltpu.VMEM((cx + 4, cy + 4, *pairs), BF),
            pltpu.VMEM((cx + 4, cy + 4, *pairs), BF),
            pltpu.VMEM(((cx + 2) * uy * 2 * kz, LANES), F32),
            pltpu.VMEM(((cx + 2) * uy * 2 * kz, LANES), F32),
            pltpu.VMEM((cx + 2, uy, *pairs), BF),
            pltpu.VMEM((cx + 2, uy, *pairs), BF),
            pltpu.VMEM((cx, cy, *pairs), F32),
            pltpu.VMEM((cx * cy * kz, 2 * chan), BF),
            pltpu.VMEM(w_second.shape, F32),
            pltpu.VMEM(w_first.shape, F32),
            pltpu.VMEM((cx, cy, 2 * kz, chan), BF),
            pltpu.VMEM((4 * taps // 3 * chan, 2 * chan), BF),
            pltpu.SemaphoreType.DMA(()),
        ],
        scalars=1,
        out_hbm=(0,),
        limit=32,
    )(side, field, up, tile, left, right, inner_x, outer_x, inner, outer, w1, b_first.reshape(1, -1), w2, b_second.reshape(1, -1), second_taps)
    sent, kept = sent.reshape(-1, chan), kept.reshape(-1, chan)
    cut = kept.shape[0] // CHAINS
    total = []
    for i in range(CHAINS):
        span = slice(i * cut, (i + 1) * cut)
        total.append(kept[span] + swap(sent[span], core).astype(F32))
    own = summed_everywhere(total, levels[1:])
    other = [swap(part_of, core) for part_of in own]
    halves_of = chan // 2, w_first.shape[1] // 2
    (squares,) = local_call(
        part(squares_body, taps, halves_of), "squares", [shape((2, 8, LANES), F32)]
    )(*own)
    step_second, step_first = local_call(
        part(norm_body, CHAINS),
        "normalize",
        [shape(w_second.shape, F32), shape(w_first.shape, F32)],
        [
            pltpu.VMEM(w_second.shape, F32),
            pltpu.VMEM(w_first.shape, F32),
            pltpu.SemaphoreType.DMA((6,)),
        ],
        scalars=1,
        out_hbm=(0, 1),
    )(side, squares, *own, *other)
    return (features, step_first, step_second)


def solution(mesh):
    in_specs = (
        P("gx", "gy", None, None),
        P("gx", "gy", None),
        P(),
        P(),
        P(),
        P(),
        P("gx", "gy", None, None),
    )
    out_specs = (P("gx", "gy", None, None), P(), P())
    return jax.shard_map(
        on_device, mesh=mesh, in_specs=in_specs, out_specs=out_specs, check_vma=False
    )
```
